128 devices in a mesh: seq: 64 (over z, y, x), exp: 2 (over core).
Axes of the slice: x: 4, y: 4, z: 4, core: 2. Of those that a mesh axis runs over, the one named last changes fastest.
Arguments:
- queries: bfloat16 [16384, 1024], P('seq', 'exp'), may hold values from -170 to 170
- keys: bfloat16 [16384, 1024], P('seq', 'exp'), may hold values from -5 to 5
- values: bfloat16 [16384, 1024], P('seq', 'exp'), may hold values from -6 to 6
- resid: bfloat16 [16384, 2048], P(('seq', 'exp')), may hold values from -6 to 6
- pair_ids: int32 [16384], replicated, may hold values from 0 to 63, never falling along the last dimension, each value on 1 to 512 neighbouring positions
- out_weight: bfloat16 [1024, 2048], P('exp'), may hold values from -0.1875 to 0.1875
- norm_gain: float32 [2048], replicated, may hold values from 0.5 to 1.5
- experts: int32 [16384, 6], P(('seq', 'exp')), may hold values from 0 to 63, all different within a row; in each aligned block of 128 rows (0 to 127, 128 to 255, ...) at most 24 rows name the same one
- gates: float32 [16384, 6], P(('seq', 'exp')), may hold values from 0.05 to 0.5
- w_gate: bfloat16 [64, 2048, 704], P('seq', None, 'exp'), may hold values from -0.125 to 0.125
- w_up: bfloat16 [64, 2048, 704], P('seq', None, 'exp'), may hold values from -0.125 to 0.125
- w_down: bfloat16 [64, 704, 2048], P('seq', 'exp'), may hold values from -0.21875 to 0.21875
Outputs:
- mixed: bfloat16 [16384, 2048], P(('seq', 'exp'))
The draws below stay inside these ranges and needn't reach their ends.
Inputs may be any that keep to these rules, and one draw needn't show every extreme that they name: In the aligned blocks of 128 rows no expert is named more than 24 times, a bound that some block reaches; each row names 6 different experts. `pair_ids`: pair numbers never fall along the sequence; each pair has 1 to 512 tokens, one exactly that many.
All inputs are finite; a program needn't handle non-finite values.
Results may differ from the reference program's by a relative error of at most 0.012.
Values may be sent and summed in bfloat16 or wider, within the bound.
A program may use at most 128 MiB of HBM per device.

```python
import math
import jax
import jax.numpy as jnp
import numpy as np
from jax import lax

D = 2048
HEADS = 8
HD = 128
FF = 704
TOP = 6
TOK_DEV = 256
EXPERTS = 64
TOKENS = 16384
WIN = 256
MOE_ROWS = 128
CAP = 24


def query_key_pair(key):
    base = jax.random.fold_in(key, 7101)
    width = HEADS * HD
    key_draw = jnp.clip(jax.random.normal(jax.random.fold_in(base, 1), (TOKENS, width), jnp.float32), -4.0, 4.0)
    query_draw = jnp.clip(jax.random.normal(jax.random.fold_in(base, 2), (TOKENS, width), jnp.float32), -4.0, 4.0)
    return (query_draw, key_draw)


def draw_queries(key, part):
    return query_key_pair(key)[0].astype(jnp.bfloat16)


def draw_keys(key, part):
    return query_key_pair(key)[1].astype(jnp.bfloat16)


def block_levels(stream_key, shape, pieces, low, high):
    factor_of, own = 1.0, jax.random.fold_in(stream_key, 6)
    for dim, blocks in pieces:
        heights = jnp.exp(jax.random.uniform(jax.random.fold_in(own, dim), (blocks,), jnp.float32, low / len(pieces), high / len(pieces)))
        factor_of = factor_of * jnp.repeat(heights, shape[dim] // blocks).reshape([-1 if axis == dim else 1 for axis in range(len(shape))])
    return factor_of


def split_up(number_of, total, reach, slope):
    loads = [(1 << 20) // math.isqrt(rank ** slope) + 1 for rank in range(2, number_of + 1)]
    rest, given = total - reach - (number_of - 1), [1] * (number_of - 1)
    while rest > 0:
        candidates = [i for i in range(number_of - 1) if given[i] < reach]
        mass, remaining = sum([loads[i] for i in candidates]), rest
        for i in candidates:
            extra = min(reach - given[i], max(1, remaining * loads[i] // mass), rest)
            given[i] = given[i] + extra
            rest = rest - extra
    return np.array([reach] + given)


def uneven(stream_key, amount, total, reach, lean):
    if amount == 2:
        one = jax.random.randint(stream_key, (), max(1, total - reach), min(reach, total - 1) + 1)
        return jnp.stack([one, total - one])
    lengths = jnp.asarray(split_up(amount, total, reach, lean), jnp.int32)
    pairs = (amount - 1) // 2
    giver, sink = lengths[1:1 + 2 * pairs:2], lengths[2:2 + 2 * pairs:2]
    margin = jnp.minimum(giver - 1, reach - sink)
    moved = jax.random.randint(jax.random.fold_in(stream_key, 1), (pairs,), 0, 1 << 20) % (margin + 1)
    lengths = lengths.at[1:1 + 2 * pairs:2].set(giver - moved).at[2:2 + 2 * pairs:2].set(sink + moved)
    return lengths[jax.random.permutation(jax.random.fold_in(stream_key, 2), amount)]


def assign_block(key, own, number, rows, count, top, limit, skew):
    sequence = jax.random.permutation(key, count)
    heavy_load, usual = portions_of(count, rows * top, limit, skew, True), portions_of(count, rows * top, limit, skew, False)
    places = jnp.arange(count)

    def named(sizes, rotation):
        used = int((sizes > 0).sum())
        fixed = max(1, used // 4)
        shifted = fixed + (places - fixed + rotation * (used - fixed)) % max(1, count - fixed)
        return jnp.zeros((count,), jnp.int32).at[sequence[jnp.where(places < fixed, places, shifted)]].set(jnp.asarray(sizes, jnp.int32))

    sizes = jnp.where(number % 4 == 0, named(heavy_load, number // 4), named(usual, number - number // 4 - 1))
    mixed = jax.random.permutation(jax.random.fold_in(own, 3), count)
    donor, receiver = mixed[0:count // 2 * 2:2], mixed[1:count // 2 * 2:2]
    room = jnp.minimum(sizes[donor] - 1, limit - sizes[receiver]) // 2
    room = jnp.where((donor == sequence[0]) | (receiver == sequence[0]) | (sizes[receiver] == 0), 0, jnp.maximum(room, 0))
    shifted = jax.random.randint(jax.random.fold_in(own, 4), (count // 2,), 0, 1 << 20) % (room + 1)
    sizes = sizes.at[donor].add(-shifted).at[receiver].add(shifted)
    labels = jnp.searchsorted(jnp.cumsum(sizes), jnp.arange(rows * top), side="right").astype(jnp.int32)
    grid = labels.reshape(top, rows).T
    grid = grid[jax.random.permutation(jax.random.fold_in(own, 1), rows)]
    rotation = jax.random.randint(jax.random.fold_in(own, 2), (rows, 1), 0, top)
    return jnp.take_along_axis(grid, (jnp.arange(top)[None, :] + rotation) % top, axis=1)


def portions_of(count, total, limit, lean, full):
    loads = [(1 << 20) // math.isqrt(grade ** lean) + 1 for grade in range(1, count + 1)]
    largest = limit if full else min(limit, max(-(-total // count), total * loads[0] // sum(loads)))
    least = 1 if total - largest >= count - 1 else 0
    given, surplus = [largest] + [least] * (count - 1), total - largest - least * (count - 1)
    while surplus > 0:
        free = [i for i in range(1, count) if given[i] < largest] or [i for i in range(1, count) if given[i] < limit]
        mass, budget = sum([loads[i] for i in free]), surplus
        for i in free:
            extra = min(limit - given[i], max(1, budget * loads[i] // mass), surplus)
            given[i] = given[i] + extra
            surplus = surplus - extra
    return np.array(given)


def gaussian(stream_key, dims, spread, limit, split=(), kind=jnp.bfloat16):
    values = spread * jax.random.normal(stream_key, dims, jnp.float32)
    if split:
        values = values * block_levels(stream_key, dims, split, -0.22, 0.18)
    return jnp.clip(values, -limit, limit).astype(kind)


def setup_inputs(seed: int = 0) -> dict:
    splits = jax.random.split(jax.random.key(seed), 13)
    queries = draw_queries(jax.random.fold_in(splits[12], 71), 0)
    keys = draw_keys(jax.random.fold_in(splits[12], 71), 0)
    values = gaussian(splits[2], (TOKENS, HEADS * HD), 1.0, 6.0, ((0, 64), (1, 2)))
    resid = gaussian(splits[3], (TOKENS, D), 1.0, 6.0, ((0, 128),))
    pair_ids = jnp.searchsorted(jnp.cumsum(uneven(splits[4], TOKENS // TOK_DEV, TOKENS, 2 * TOK_DEV, 2)), jnp.arange(TOKENS), side="right").astype(jnp.int32)
    out_weight = gaussian(splits[5], (HEADS * HD, D), (HEADS * HD) ** -0.5, 0.1875, ((0, 2),))
    norm_gain = jnp.clip(1.0 + 0.1 * jax.random.normal(splits[6], (D,), jnp.float32), 0.5, 1.5)
    experts_keys = jax.random.split(jax.random.fold_in(splits[7], 1), TOKENS // MOE_ROWS)
    experts_turns = jax.random.permutation(jax.random.fold_in(splits[7], 3), TOKENS // MOE_ROWS)
    experts = jax.vmap(lambda own, number: assign_block(jax.random.fold_in(splits[7], 2), own, number, MOE_ROWS, EXPERTS, TOP, CAP, 2))(experts_keys, experts_turns).reshape((TOKENS, TOP))
    gates = jnp.clip(0.05 + 0.45 * jax.random.uniform(splits[8], (TOKENS, TOP), jnp.float32) ** block_levels(splits[8], (TOKENS, TOP), ((0, 128),), -0.2, 0.2), 0.05, 0.5)
    w_gate = gaussian(splits[9], (EXPERTS, D, FF), D ** -0.5, 0.125, ((0, 64), (2, 2)))
    w_up = gaussian(splits[10], (EXPERTS, D, FF), D ** -0.5, 0.125, ((0, 64), (2, 2)))
    w_down = gaussian(splits[11], (EXPERTS, FF, D), FF ** -0.5, 0.21875, ((0, 64), (1, 2)))
    return {"queries": queries, "keys": keys, "values": values, "resid": resid, "pair_ids": pair_ids, "out_weight": out_weight, "norm_gain": norm_gain, "experts": experts, "gates": gates, "w_gate": w_gate, "w_up": w_up, "w_down": w_down}


def attend(query_block, key_block, value_block, query_ids, key_ids, query_pos, key_pos):
    rows = query_block.shape[0]
    span = key_block.shape[0]
    qh = query_block.astype(jnp.float32).reshape(rows, HEADS, HD)
    kh = key_block.astype(jnp.float32).reshape(span, HEADS, HD)
    vh = value_block.astype(jnp.float32).reshape(span, HEADS, HD)
    score = jnp.einsum('qhd,khd->hqk', qh, kh) / math.sqrt(HD)
    allowed = (query_ids[:, None] == key_ids[None, :]) & (jnp.abs(query_pos[:, None] - key_pos[None, :]) < WIN)
    score = jnp.where(allowed[None], score, -jnp.inf)
    top = lax.optimization_barrier(jnp.max(score, axis=-1, keepdims=True))
    weights = jnp.exp(score - top)
    probs = (weights / lax.optimization_barrier(jnp.sum(weights, axis=-1, keepdims=True))).astype(jnp.bfloat16)
    outcome = jnp.einsum('hqk,khd->qhd', probs.astype(jnp.float32), vh)
    return outcome.reshape(rows, HEADS * HD).astype(jnp.bfloat16)

def reference(queries, keys, values, resid, pair_ids, out_weight, norm_gain, experts, gates, w_gate, w_up, w_down):
    key_pad = jnp.pad(keys, ((WIN, WIN), (0, 0)))
    value_pad = jnp.pad(values, ((WIN, WIN), (0, 0)))
    id_pad = jnp.pad(pair_ids, (WIN, WIN), constant_values=-1)

    def block(index):
        start = index * TOK_DEV
        query_block = lax.dynamic_slice_in_dim(queries, start, TOK_DEV, 0)
        key_block = lax.dynamic_slice_in_dim(key_pad, start, TOK_DEV + 2 * WIN, 0)
        value_block = lax.dynamic_slice_in_dim(value_pad, start, TOK_DEV + 2 * WIN, 0)
        query_ids = lax.dynamic_slice_in_dim(pair_ids, start, TOK_DEV, 0)
        key_ids = lax.dynamic_slice_in_dim(id_pad, start, TOK_DEV + 2 * WIN, 0)
        query_pos = jnp.arange(TOK_DEV, dtype=jnp.int32) + WIN
        key_pos = jnp.arange(TOK_DEV + 2 * WIN, dtype=jnp.int32)
        return attend(query_block, key_block, value_block, query_ids, key_ids, query_pos, key_pos)
    attended = lax.map(block, jnp.arange(TOKENS // TOK_DEV, dtype=jnp.int32)).reshape(TOKENS, HEADS * HD)
    stream = resid.astype(jnp.float32) + jnp.dot(attended, out_weight, preferred_element_type=jnp.float32)
    meansq = lax.optimization_barrier(jnp.mean(stream * stream, axis=-1, keepdims=True))
    normed = (stream * lax.rsqrt(meansq + 1e-05) * norm_gain).astype(jnp.bfloat16)
    flat_experts = experts.reshape(-1).astype(jnp.int32)
    flat_gates = gates.reshape(-1)
    order = jnp.argsort(flat_experts, stable=True).astype(jnp.int32)
    counts = lax.optimization_barrier(jnp.sum((flat_experts[:, None] == jnp.arange(EXPERTS, dtype=jnp.int32)[None, :]).astype(jnp.int32), axis=0))
    starts = (jnp.cumsum(counts) - counts).astype(jnp.int32)
    bound = TOKENS // MOE_ROWS * CAP
    order_pad = jnp.concatenate([order, jnp.zeros((bound,), jnp.int32)])

    def per_expert(total, expert):
        picks = lax.dynamic_slice_in_dim(order_pad, starts[expert], bound, 0)
        valid = jnp.arange(bound, dtype=jnp.int32) < counts[expert]
        token_rows = picks // TOP
        inputs = normed[token_rows]
        gate_part = jnp.dot(inputs, w_gate[expert], preferred_element_type=jnp.float32)
        up_part = jnp.dot(inputs, w_up[expert], preferred_element_type=jnp.float32)
        act = (jax.nn.silu(gate_part) * up_part).astype(jnp.bfloat16)
        result = jnp.dot(act, w_down[expert], preferred_element_type=jnp.float32).astype(jnp.bfloat16)
        weight = jnp.where(valid, flat_gates[picks], jnp.zeros((), flat_gates.dtype))
        total = total.at[token_rows].add(result.astype(jnp.float32) * weight[:, None])
        return (total, None)
    mixture, unused = lax.scan(per_expert, jnp.zeros((TOKENS, D), jnp.float32), jnp.arange(EXPERTS, dtype=jnp.int32))
    return (stream + mixture).astype(jnp.bfloat16)
```

```python
import math

import jax
import jax.numpy as jnp
from jax import lax
from jax.sharding import PartitionSpec as P

HD = 128
TOP = 6
SWAP = [(0, 1), (1, 0)]


def with_halo(cells, axis, dim, width):
    count = lax.axis_size(axis)
    ends = count - 1
    head = lax.slice_in_dim(cells, 0, width, axis=dim)
    tail = lax.slice_in_dim(cells, cells.shape[dim] - width, cells.shape[dim], axis=dim)
    return jnp.concatenate(
        [
            lax.ppermute(tail, axis, [(i, (i + 1) % count) for i in range(ends)]),
            cells,
            lax.ppermute(head, axis, [((i + 1) % count, i) for i in range(ends)]),
        ],
        axis=dim,
    )


def swap(block):
    return lax.ppermute(block, "exp", SWAP)


def attention(queries, keys, values, pair_ids):
    tok_rows, local_width = queries.shape
    local_heads = local_width // HD
    shard = lax.axis_index("seq")
    widened = with_halo(jnp.stack([keys, values]), "seq", 1, tok_rows)
    id_pad = jnp.pad(pair_ids, (tok_rows, tok_rows), constant_values=-1)
    key_ids = lax.dynamic_slice_in_dim(id_pad, shard * tok_rows, 3 * tok_rows, 0)
    query_ids = lax.dynamic_slice_in_dim(id_pad, shard * tok_rows + tok_rows, tok_rows, 0)
    query_pos = jnp.arange(tok_rows, dtype=jnp.int32) + tok_rows
    key_pos = jnp.arange(3 * tok_rows, dtype=jnp.int32)
    allowed = (query_ids[:, None] == key_ids[None, :]) & (
        jnp.abs(query_pos[:, None] - key_pos[None, :]) < tok_rows
    )
    query_heads = queries.reshape(tok_rows, local_heads, HD)
    key_heads = widened[0].reshape(3 * tok_rows, local_heads, HD)
    value_heads = widened[1].reshape(3 * tok_rows, local_heads, HD)
    score = jnp.einsum(
        "qhd,khd->hqk", query_heads, key_heads, preferred_element_type=jnp.float32
    ) / math.sqrt(HD)
    score = jnp.where(allowed[None], score, -jnp.inf)
    top = jnp.max(score, axis=-1, keepdims=True)
    weights = jnp.exp(score - top)
    probs = (weights / jnp.sum(weights, axis=-1, keepdims=True)).astype(jnp.bfloat16)
    attended = jnp.einsum("hqk,khd->qhd", probs, value_heads, preferred_element_type=jnp.float32)
    return attended.reshape(tok_rows, local_width).astype(jnp.bfloat16)


def routing(experts, gates, n_experts, capacity):
    rows = experts.shape[0]
    names = jnp.arange(n_experts, dtype=jnp.int32)
    hits = experts[:, :, None] == names[None, None, :]
    named = jnp.sum(hits.astype(jnp.float32), axis=1)
    weight = jnp.sum(jnp.where(hits, gates[:, :, None], 0.0), axis=1)
    order = jnp.arange(rows, dtype=jnp.int32)
    before = (order[None, :] < order[:, None]).astype(jnp.bfloat16)
    ranks = jnp.dot(before, named.astype(jnp.bfloat16), preferred_element_type=jnp.float32)
    ranks = jnp.where(named > 0.0, ranks, -1.0)
    slots = jnp.arange(capacity, dtype=jnp.int32).astype(jnp.float32)
    chosen = ranks.T[:, None, :] == slots[None, :, None]
    pick = jnp.where(chosen, 1.0, 0.0).reshape(n_experts * capacity, rows).astype(jnp.bfloat16)
    blend = jnp.where(chosen, weight.T[:, None, :], 0.0)
    blend = blend.reshape(n_experts * capacity, rows).astype(jnp.bfloat16)
    return pick, blend


def shards(
    queries,
    keys,
    values,
    resid,
    pair_ids,
    out_weight,
    norm_gain,
    experts,
    gates,
    w_gate,
    w_up,
    w_down,
):
    moe_rows = resid.shape[0]
    n_experts = lax.axis_size("seq") * w_gate.shape[0]
    capacity = 2 * moe_rows * TOP // n_experts
    core = lax.axis_index("exp")
    attended = attention(queries, keys, values, pair_ids)
    mine = lax.dynamic_slice_in_dim(attended, core * moe_rows, moe_rows, 0)
    yours = swap(lax.dynamic_slice_in_dim(attended, (1 - core) * moe_rows, moe_rows, 0))
    out_other = swap(out_weight)
    gate_other, up_other, down_other = swap(w_gate[0]), swap(w_up[0]), swap(w_down[0])
    stream = (
        resid.astype(jnp.float32)
        + jnp.dot(mine, out_weight, preferred_element_type=jnp.float32)
        + jnp.dot(yours, out_other, preferred_element_type=jnp.float32)
    )
    meansq = jnp.mean(stream * stream, axis=-1, keepdims=True)
    normed = (stream * lax.rsqrt(meansq + 1e-05) * norm_gain).astype(jnp.bfloat16)
    pick, blend = routing(experts, gates, n_experts, capacity)
    outgoing = jnp.dot(pick, normed, preferred_element_type=jnp.float32).astype(jnp.bfloat16)
    outgoing = outgoing.reshape(n_experts, capacity, normed.shape[1])
    arrived = lax.all_to_all(outgoing, "seq", split_axis=0, concat_axis=0, tiled=True)
    inputs = arrived.reshape(n_experts * capacity, arrived.shape[2])

    def half(w_g, w_u, w_d):
        gate_part = jnp.dot(inputs, w_g, preferred_element_type=jnp.float32)
        up_part = jnp.dot(inputs, w_u, preferred_element_type=jnp.float32)
        act = (jax.nn.silu(gate_part) * up_part).astype(jnp.bfloat16)
        return jnp.dot(act, w_d, preferred_element_type=jnp.float32)

    result = half(w_gate[0], w_up[0], w_down[0]) + half(gate_other, up_other, down_other)
    result = result.astype(jnp.bfloat16).reshape(n_experts, capacity, arrived.shape[2])
    back = lax.all_to_all(result, "seq", split_axis=0, concat_axis=0, tiled=True)
    back = back.reshape(n_experts * capacity, back.shape[2])
    mixture = lax.dot_general(
        blend, back, (((0,), (0,)), ((), ())), preferred_element_type=jnp.float32
    )
    return (stream + mixture).astype(jnp.bfloat16)


def solution(mesh):
    in_specs = (
        P("seq", "exp"),
        P("seq", "exp"),
        P("seq", "exp"),
        P(("seq", "exp"), None),
        P(),
        P("exp", None),
        P(),
        P(("seq", "exp"), None),
        P(("seq", "exp"), None),
        P("seq", None, "exp"),
        P("seq", None, "exp"),
        P("seq", "exp", None),
    )
    out_specs = P(("seq", "exp"), None)
    return jax.shard_map(shards, mesh=mesh, in_specs=in_specs, out_specs=out_specs, check_vma=False)
```

```python
import math

import jax
import jax.numpy as jnp
from jax import lax
from jax.experimental import pallas as pl
from jax.experimental.pallas import tpu as pltpu
from jax.sharding import PartitionSpec as P

HD = 128
TOP = 6
SWAP = [(0, 1), (1, 0)]
SIDE = 4
AXES = ("z", "y", "x")
ORDERS = ((2, 1, 0), (1, 0, 2), (0, 2, 1))


def with_halo(cells, axis, dim, width):
    count = lax.axis_size(axis)
    ends = count - 1
    head = lax.slice_in_dim(cells, 0, width, axis=dim)
    tail = lax.slice_in_dim(cells, cells.shape[dim] - width, cells.shape[dim], axis=dim)
    return jnp.concatenate(
        [
            lax.ppermute(tail, axis, [(i, (i + 1) % count) for i in range(ends)]),
            cells,
            lax.ppermute(head, axis, [((i + 1) % count, i) for i in range(ends)]),
        ],
        axis=dim,
    )


def swap(block):
    return lax.ppermute(block, "exp", SWAP)


def peer(axis, delta):
    me = lax.axis_index("seq")
    at = [me // (SIDE * SIDE), (me // SIDE) % SIDE, me % SIDE]
    at[axis] = (at[axis] + delta) % SIDE
    return ((at[0] * SIDE + at[1]) * SIDE + at[2], lax.axis_index("exp"))


def cell(group, **fixed):
    return tuple(fixed.get(AXES[i], slice(None)) for i in range(3)) + (group,)


def exchange_kernel(src, out, first, second, local_sem, send_sem, recv_sem):
    barrier = pltpu.get_barrier_semaphore()
    for axis in range(3):
        for delta in range(1, SIDE):
            pl.semaphore_signal(
                barrier, inc=1, device_id=peer(axis, delta), device_id_type=pl.DeviceIdType.MESH
            )
    pl.semaphore_wait(barrier, 3 * (SIDE - 1))

    used = [0]
    sent = []

    def send(axis, delta, source, target):
        number = used[0]
        used[0] += 1
        copy = pltpu.make_async_remote_copy(
            src_ref=source,
            dst_ref=target,
            send_sem=send_sem.at[number],
            recv_sem=recv_sem.at[number],
            device_id=peer(axis, delta),
            device_id_type=pl.DeviceIdType.MESH,
        )
        copy.start()
        sent.append(copy)
        return copy

    routes = [(g, ORDERS[g]) for g in range(3)]
    deltas = (2, 1, 3)
    one, two, three = {}, {}, []
    for d in deltas:
        for g, (a, b, c) in routes:
            na = AXES[a]
            one[g, d] = send(
                a, d, src.at[cell(g, **{na: d})], first.at[cell(g, **{na: SIDE - d})]
            )

    def relay(i, g, d):
        a, b, c = ORDERS[g]
        na, nb = AXES[a], AXES[b]
        held = src if i == 0 else first
        two[g, i, d] = send(
            b,
            d,
            held.at[cell(g, **{na: i, nb: d})],
            second.at[cell(g, **{na: i, nb: SIDE - d})],
        )

    for d in deltas:
        for g, _ in routes:
            relay(0, g, d)
    for i in (1, 3, 2):
        for g, _ in routes:
            one[g, SIDE - i].wait_recv()
        for d in deltas:
            for g, _ in routes:
                relay(i, g, d)

    def deliver(g, d, held, **at):
        c = ORDERS[g][2]
        nc = AXES[c]
        three.append(
            send(
                c,
                d,
                held.at[cell(g, **{nc: d}, **at)],
                out.at[cell(g, **{nc: SIDE - d}, **at)],
            )
        )

    locals_ = []

    def keep(g, held, **at):
        nc = AXES[ORDERS[g][2]]
        where = cell(g, **{nc: 0}, **at)
        copy = pltpu.make_async_copy(held.at[where], out.at[where], local_sem.at[len(locals_)])
        copy.start()
        locals_.append(copy)

    for i in range(SIDE):
        for d in deltas:
            for g, (a, b, c) in routes:
                deliver(g, d, src if i == 0 else first, **{AXES[a]: i, AXES[b]: 0})
    for j in (1, 3, 2):
        for i in range(SIDE):
            for g, _ in routes:
                two[g, i, SIDE - j].wait_recv()
        for d in deltas:
            for g, (a, b, c) in routes:
                deliver(g, d, second, **{AXES[b]: j})
    for g, (a, b, c) in routes:
        for i in range(SIDE):
            keep(g, src if i == 0 else first, **{AXES[a]: i, AXES[b]: 0})
        for j in range(1, SIDE):
            keep(g, second, **{AXES[b]: j})
    for copy in three:
        copy.wait_recv()
    for copy in locals_:
        copy.wait()
    for copy in sent:
        copy.wait_send()


def exchange(blocks, number):
    copies = 3 * (3 + 4 * 3 + 3 * (4 + 3))
    return pl.pallas_call(
        exchange_kernel,
        out_shape=jax.ShapeDtypeStruct(blocks.shape, blocks.dtype),
        in_specs=[pl.BlockSpec(memory_space=pl.ANY)],
        out_specs=pl.BlockSpec(memory_space=pl.ANY),
        scratch_shapes=[
            pltpu.VMEM(blocks.shape, blocks.dtype),
            pltpu.VMEM(blocks.shape, blocks.dtype),
            pltpu.SemaphoreType.DMA((3 * (4 + 3),)),
            pltpu.SemaphoreType.DMA((copies,)),
            pltpu.SemaphoreType.DMA((copies,)),
        ],
        compiler_params=pltpu.CompilerParams(
            collective_id=number, has_side_effects=True, vmem_limit_bytes=20 << 20
        ),
        name="exchange_%d" % number,
    )(blocks)


def attention(queries, keys, values, pair_ids):
    tok_rows, local_width = queries.shape
    local_heads = local_width // HD
    shard = lax.axis_index("seq")
    widened = with_halo(jnp.stack([keys, values]), "seq", 1, tok_rows)
    id_pad = jnp.pad(pair_ids, (tok_rows, tok_rows), constant_values=-1)
    key_ids = lax.dynamic_slice_in_dim(id_pad, shard * tok_rows, 3 * tok_rows, 0)
    query_ids = lax.dynamic_slice_in_dim(id_pad, shard * tok_rows + tok_rows, tok_rows, 0)
    query_pos = jnp.arange(tok_rows, dtype=jnp.int32) + tok_rows
    key_pos = jnp.arange(3 * tok_rows, dtype=jnp.int32)
    allowed = (query_ids[:, None] == key_ids[None, :]) & (
        jnp.abs(query_pos[:, None] - key_pos[None, :]) < tok_rows
    )
    query_heads = queries.reshape(tok_rows, local_heads, HD)
    key_heads = widened[0].reshape(3 * tok_rows, local_heads, HD)
    value_heads = widened[1].reshape(3 * tok_rows, local_heads, HD)
    score = jnp.einsum(
        "qhd,khd->hqk", query_heads, key_heads, preferred_element_type=jnp.float32
    ) / math.sqrt(HD)
    score = jnp.where(allowed[None], score, -jnp.inf)
    top = jnp.max(score, axis=-1, keepdims=True)
    weights = jnp.exp(score - top)
    probs = (weights / jnp.sum(weights, axis=-1, keepdims=True)).astype(jnp.bfloat16)
    attended = jnp.einsum("hqk,khd->qhd", probs, value_heads, preferred_element_type=jnp.float32)
    return attended.reshape(tok_rows, local_width).astype(jnp.bfloat16)


def routing(experts, gates, n_experts, capacity):
    rows = experts.shape[0]
    step = jnp.arange(n_experts, dtype=jnp.int32)
    me = lax.axis_index("seq")
    names = (
        (step // 16 + me // 16) % SIDE * 16
        + (step // 4 % SIDE + me // 4 % SIDE) % SIDE * 4
        + (step % SIDE + me % SIDE) % SIDE
    )
    hits = experts[:, :, None] == names[None, None, :]
    named = jnp.sum(hits.astype(jnp.float32), axis=1)
    weight = jnp.sum(jnp.where(hits, gates[:, :, None], 0.0), axis=1)
    order = jnp.arange(rows, dtype=jnp.int32)
    before = (order[None, :] < order[:, None]).astype(jnp.bfloat16)
    ranks = jnp.dot(before, named.astype(jnp.bfloat16), preferred_element_type=jnp.float32)
    ranks = jnp.where(named > 0.0, ranks, -1.0)
    slots = jnp.arange(capacity, dtype=jnp.int32).astype(jnp.float32)
    chosen = ranks.T[:, None, :] == slots[None, :, None]
    pick = jnp.where(chosen, 1.0, 0.0).reshape(n_experts * capacity, rows).astype(jnp.bfloat16)
    blend = jnp.where(chosen, weight.T[:, None, :], 0.0)
    blend = blend.reshape(n_experts * capacity, rows).astype(jnp.bfloat16)
    return pick, blend


def shards(
    queries,
    keys,
    values,
    resid,
    pair_ids,
    out_weight,
    norm_gain,
    experts,
    gates,
    w_gate,
    w_up,
    w_down,
):
    moe_rows = resid.shape[0]
    n_experts = lax.axis_size("seq") * w_gate.shape[0]
    capacity = 2 * moe_rows * TOP // n_experts
    core = lax.axis_index("exp")
    attended = attention(queries, keys, values, pair_ids)
    mine = lax.dynamic_slice_in_dim(attended, core * moe_rows, moe_rows, 0)
    yours = swap(lax.dynamic_slice_in_dim(attended, (1 - core) * moe_rows, moe_rows, 0))
    out_other = swap(out_weight)
    gate_other, up_other, down_other = swap(w_gate[0]), swap(w_up[0]), swap(w_down[0])
    stream = (
        resid.astype(jnp.float32)
        + jnp.dot(mine, out_weight, preferred_element_type=jnp.float32)
        + jnp.dot(yours, out_other, preferred_element_type=jnp.float32)
    )
    meansq = jnp.mean(stream * stream, axis=-1, keepdims=True)
    normed = (stream * lax.rsqrt(meansq + 1e-05) * norm_gain).astype(jnp.bfloat16)
    pick, blend = routing(experts, gates, n_experts, capacity)
    outgoing = jnp.dot(pick, normed, preferred_element_type=jnp.float32).astype(jnp.bfloat16)
    width = normed.shape[1]
    cells = (SIDE, SIDE, SIDE, 3, capacity // 3, width)
    arrived = exchange(outgoing.reshape(cells), 0)
    inputs = arrived.reshape(n_experts * capacity, width)
    w_g = jnp.concatenate([w_gate[0], gate_other], axis=1)
    w_u = jnp.concatenate([w_up[0], up_other], axis=1)
    w_d = jnp.concatenate([w_down[0], down_other], axis=0)
    gate_part = jnp.dot(inputs, w_g, preferred_element_type=jnp.float32)
    up_part = jnp.dot(inputs, w_u, preferred_element_type=jnp.float32)
    act = (jax.nn.silu(gate_part) * up_part).astype(jnp.bfloat16)
    result = jnp.dot(act, w_d, preferred_element_type=jnp.float32).astype(jnp.bfloat16)
    back = exchange(result.reshape(cells), 1).reshape(n_experts * capacity, width)
    mixture = lax.dot_general(
        blend, back, (((0,), (0,)), ((), ())), preferred_element_type=jnp.float32
    )
    return (stream + mixture).astype(jnp.bfloat16)


def solution(mesh):
    in_specs = (
        P("seq", "exp"),
        P("seq", "exp"),
        P("seq", "exp"),
        P(("seq", "exp"), None),
        P(),
        P("exp", None),
        P(),
        P(("seq", "exp"), None),
        P(("seq", "exp"), None),
        P("seq", None, "exp"),
        P("seq", None, "exp"),
        P("seq", "exp", None),
    )
    out_specs = P(("seq", "exp"), None)
    return jax.shard_map(shards, mesh=mesh, in_specs=in_specs, out_specs=out_specs, check_vma=False)
```

```python
import math

import jax
import jax.numpy as jnp
from jax import lax
from jax.experimental import pallas as pl
from jax.experimental.pallas import tpu as pltpu
from jax.sharding import PartitionSpec as P

HD = 128
TOP = 6
SWAP = [(0, 1), (1, 0)]
SIDE = 4
AXES = ("z", "y", "x")
ORDERS = ((2, 1, 0), (1, 0, 2), (0, 2, 1))


def with_halo(cells, axis, dim, width):
    count = lax.axis_size(axis)
    ends = count - 1
    head = lax.slice_in_dim(cells, 0, width, axis=dim)
    tail = lax.slice_in_dim(cells, cells.shape[dim] - width, cells.shape[dim], axis=dim)
    return jnp.concatenate(
        [
            lax.ppermute(tail, axis, [(i, (i + 1) % count) for i in range(ends)]),
            cells,
            lax.ppermute(head, axis, [((i + 1) % count, i) for i in range(ends)]),
        ],
        axis=dim,
    )


def swap(block):
    return lax.ppermute(block, "exp", SWAP)


def peer(axis, delta):
    me = lax.axis_index("seq")
    at = [me // (SIDE * SIDE), (me // SIDE) % SIDE, me % SIDE]
    at[axis] = (at[axis] + delta) % SIDE
    return ((at[0] * SIDE + at[1]) * SIDE + at[2], lax.axis_index("exp"))


def cell(group, **fixed):
    return tuple(fixed.get(AXES[i], slice(None)) for i in range(3)) + (group,)


def tile(group, last, **fixed):
    c = ORDERS[group][2]
    rest = tuple(fixed.get(AXES[i], slice(None)) for i in range(3) if i != c)
    return (last, group) + rest


def expert_kernel(
    src,
    gate_w,
    up_w,
    down_w,
    out,
    first,
    second,
    arrived,
    result,
    third,
    fourth,
    weights,
    rows,
    act,
    local_sem,
    send_sem,
    recv_sem,
):
    mesh_id = pl.DeviceIdType.MESH
    partner = (lax.axis_index("seq"), 1 - lax.axis_index("exp"))
    barrier = pltpu.get_barrier_semaphore()
    for axis in range(3):
        for delta in range(1, SIDE):
            pl.semaphore_signal(barrier, inc=1, device_id=peer(axis, delta), device_id_type=mesh_id)
    pl.semaphore_signal(barrier, inc=1, device_id=partner, device_id_type=mesh_id)
    pl.semaphore_wait(barrier, 3 * (SIDE - 1) + 1)

    sent = []
    moved = []

    def send_to(device, source, target):
        copy = pltpu.make_async_remote_copy(
            src_ref=source,
            dst_ref=target,
            send_sem=send_sem.at[len(sent)],
            recv_sem=recv_sem.at[len(sent)],
            device_id=device,
            device_id_type=mesh_id,
        )
        copy.start()
        sent.append(copy)
        return copy

    def send(axis, delta, source, target):
        return send_to(peer(axis, delta), source, target)

    def move(source, target):
        copy = pltpu.make_async_copy(source, target, local_sem.at[len(moved)])
        copy.start()
        moved.append(copy)
        return copy

    groups = range(3)
    deltas = (2, 1, 3)
    inward = (1, 3, 2)
    name = [[AXES[axis] for axis in order] for order in ORDERS]
    one, two, three = {}, {}, {}
    for d in deltas:
        for g in groups:
            na = name[g][0]
            one[g, d] = send(
                ORDERS[g][0],
                d,
                src.at[cell(g, **{na: d})],
                first.at[cell(g, **{na: SIDE - d})],
            )
    swapped = []
    own = []
    for i, w in enumerate((gate_w, up_w, down_w)):
        swapped.append(send_to(partner, w, weights.at[1, i]))
        own.append(move(w, weights.at[0, i]))

    def relay(i, g, d):
        na, nb, _ = name[g]
        held = src if i == 0 else first
        two[g, i, d] = send(
            ORDERS[g][1],
            d,
            held.at[cell(g, **{na: i, nb: d})],
            second.at[cell(g, **{na: i, nb: SIDE - d})],
        )

    def deliver(g, d, held, **at):
        nc = name[g][2]
        copy = send(
            ORDERS[g][2],
            d,
            held.at[cell(g, **{nc: d}, **at)],
            arrived.at[tile(g, SIDE - d, **at)],
        )
        three.setdefault(SIDE - d, []).append(copy)

    kept = []

    def keep(g, held, **at):
        nc = name[g][2]
        kept.append(move(held.at[cell(g, **{nc: 0}, **at)], arrived.at[tile(g, 0, **at)]))

    for d in deltas:
        for g in groups:
            relay(0, g, d)
    for i in inward:
        for g in groups:
            one[g, SIDE - i].wait_recv()
        for d in deltas:
            for g in groups:
                relay(i, g, d)
    for i in range(SIDE):
        for d in inward:
            for g in groups:
                na, nb, _ = name[g]
                deliver(g, d, src if i == 0 else first, **{na: i, nb: 0})
        for g in groups:
            na, nb, _ = name[g]
            keep(g, src if i == 0 else first, **{na: i, nb: 0})
    for j in inward:
        for i in range(SIDE):
            for g in groups:
                two[g, i, SIDE - j].wait_recv()
        for d in inward:
            for g in groups:
                deliver(g, d, second, **{name[g][1]: j})
        for g in groups:
            keep(g, second, **{name[g][1]: j})

    for copy in swapped:
        copy.wait_recv()
    for copy in own + kept:
        copy.wait()

    batch = rows.shape[0]
    width = rows.shape[1]
    chunk = 512
    contract = (((1,), (1,)), ((), ()))

    def ffn(j):
        rows[...] = arrived[j].astype(jnp.float32).reshape(batch, width).astype(jnp.bfloat16)

        @pl.loop(0, 2)
        def _(h):
            gate = lax.dot_general(
                rows[...], weights[h, 0], contract, preferred_element_type=jnp.float32
            )
            up = lax.dot_general(
                rows[...], weights[h, 1], contract, preferred_element_type=jnp.float32
            )
            act[h] = (gate / (1.0 + jnp.exp(-gate)) * up).astype(jnp.bfloat16)

        for n in range(0, width, chunk):
            cols = slice(n, n + chunk)
            total = jnp.dot(act[0], weights[0, 2, :, cols], preferred_element_type=jnp.float32)
            total += jnp.dot(act[1], weights[1, 2, :, cols], preferred_element_type=jnp.float32)
            total = total.reshape(result.shape[1:5] + (chunk,))
            result[j, :, :, :, :, cols] = total.astype(jnp.bfloat16)

    back_one, back_two, back_three = {}, {}, []

    def back_relay(j, g):
        held = result if j == 0 else third
        nb = name[g][1]
        for d in deltas:
            back_two[g, j, d] = send(
                ORDERS[g][1],
                d,
                held.at[tile(g, j, **{nb: d})],
                fourth.at[tile(g, j, **{nb: SIDE - d})],
            )

    def back_direct(j, g):
        held = result if j == 0 else third
        na, nb, nc = name[g]
        for d in deltas:
            back_three.append(
                send(
                    ORDERS[g][0],
                    d,
                    held.at[tile(g, j, **{na: d, nb: 0})],
                    out.at[cell(g, **{na: SIDE - d, nb: 0, nc: j})],
                )
            )
        move(held.at[tile(g, j, **{na: 0, nb: 0})], out.at[cell(g, **{na: 0, nb: 0, nc: j})])

    for j in (0,) + inward:
        for copy in three.get(j, ()):
            copy.wait_recv()
        ffn(j)
        for g in groups:
            if j:
                back_one[g, j] = send(
                    ORDERS[g][2], j, result.at[tile(g, j)], third.at[tile(g, SIDE - j)]
                )
            else:
                back_relay(0, g)
    for g in groups:
        back_direct(0, g)
    for j in (3, 1, 2):
        for g in groups:
            back_one[g, SIDE - j].wait_recv()
            back_relay(j, g)
        for g in groups:
            back_direct(j, g)
    for b in inward:
        for g in groups:
            for j in range(SIDE):
                back_two[g, j, SIDE - b].wait_recv()
        for g in groups:
            na, nb, _ = name[g]
            for d in deltas:
                back_three.append(
                    send(
                        ORDERS[g][0],
                        d,
                        fourth.at[tile(g, slice(None), **{na: d, nb: b})],
                        out.at[cell(g, **{na: SIDE - d, nb: b})],
                    )
                )
            move(
                fourth.at[tile(g, slice(None), **{na: 0, nb: b})],
                out.at[cell(g, **{na: 0, nb: b})],
            )
    for copy in back_three:
        copy.wait_recv()
    for copy in moved[len(own) + len(kept) :]:
        copy.wait()
    for copy in sent:
        copy.wait_send()


def run_experts(blocks, gate_w, up_w, down_w):
    dtype = blocks.dtype
    by_last = (SIDE, 3, SIDE, SIDE) + blocks.shape[4:]
    batch = 3 * SIDE * SIDE * blocks.shape[4]
    hidden, width = down_w.shape
    copies = 2 * 3 * (3 + 4 * 3 + 3 * (4 + 3)) + 3
    return pl.pallas_call(
        expert_kernel,
        out_shape=jax.ShapeDtypeStruct(blocks.shape, dtype),
        in_specs=[pl.BlockSpec(memory_space=pl.ANY)] * 4,
        out_specs=pl.BlockSpec(memory_space=pl.ANY),
        scratch_shapes=[
            pltpu.VMEM(blocks.shape, dtype),
            pltpu.VMEM(blocks.shape, dtype),
            pltpu.VMEM(by_last, dtype),
            pltpu.VMEM(by_last, dtype),
            pltpu.VMEM(by_last, dtype),
            pltpu.VMEM(by_last, dtype),
            pltpu.VMEM((2, 3, hidden, width), dtype),
            pltpu.VMEM((batch, width), dtype),
            pltpu.VMEM((2, batch, hidden), dtype),
            pltpu.SemaphoreType.DMA((3 + 2 * 3 * (4 + 3),)),
            pltpu.SemaphoreType.DMA((copies,)),
            pltpu.SemaphoreType.DMA((copies,)),
        ],
        compiler_params=pltpu.CompilerParams(
            collective_id=0, has_side_effects=True, vmem_limit_bytes=60 << 20
        ),
        name="run_experts",
    )(blocks, gate_w, up_w, down_w)


def attention(queries, keys, values, pair_ids):
    tok_rows, local_width = queries.shape
    local_heads = local_width // HD
    shard = lax.axis_index("seq")
    widened = with_halo(jnp.stack([keys, values]), "seq", 1, tok_rows)
    id_pad = jnp.pad(pair_ids, (tok_rows, tok_rows), constant_values=-1)
    key_ids = lax.dynamic_slice_in_dim(id_pad, shard * tok_rows, 3 * tok_rows, 0)
    query_ids = lax.dynamic_slice_in_dim(id_pad, shard * tok_rows + tok_rows, tok_rows, 0)
    query_pos = jnp.arange(tok_rows, dtype=jnp.int32) + tok_rows
    key_pos = jnp.arange(3 * tok_rows, dtype=jnp.int32)
    allowed = (query_ids[:, None] == key_ids[None, :]) & (
        jnp.abs(query_pos[:, None] - key_pos[None, :]) < tok_rows
    )
    query_heads = queries.reshape(tok_rows, local_heads, HD)
    key_heads = widened[0].reshape(3 * tok_rows, local_heads, HD)
    value_heads = widened[1].reshape(3 * tok_rows, local_heads, HD)
    score = jnp.einsum(
        "qhd,khd->hqk", query_heads, key_heads, preferred_element_type=jnp.float32
    ) / math.sqrt(HD)
    score = jnp.where(allowed[None], score, -jnp.inf)
    top = jnp.max(score, axis=-1, keepdims=True)
    weights = jnp.exp(score - top)
    probs = (weights / jnp.sum(weights, axis=-1, keepdims=True)).astype(jnp.bfloat16)
    attended = jnp.einsum("hqk,khd->qhd", probs, value_heads, preferred_element_type=jnp.float32)
    return attended.reshape(tok_rows, local_width).astype(jnp.bfloat16)


def routing(experts, gates, n_experts, capacity):
    rows = experts.shape[0]
    step = jnp.arange(n_experts, dtype=jnp.int32)
    me = lax.axis_index("seq")
    names = (
        (step // 16 + me // 16) % SIDE * 16
        + (step // 4 % SIDE + me // 4 % SIDE) % SIDE * 4
        + (step % SIDE + me % SIDE) % SIDE
    )
    hits = experts[:, :, None] == names[None, None, :]
    named = jnp.sum(hits.astype(jnp.float32), axis=1)
    weight = jnp.sum(jnp.where(hits, gates[:, :, None], 0.0), axis=1)
    order = jnp.arange(rows, dtype=jnp.int32)
    before = (order[None, :] < order[:, None]).astype(jnp.bfloat16)
    ranks = jnp.dot(before, named.astype(jnp.bfloat16), preferred_element_type=jnp.float32)
    ranks = jnp.where(named > 0.0, ranks, -1.0)
    slots = jnp.arange(capacity, dtype=jnp.int32).astype(jnp.float32)
    chosen = ranks.T[:, None, :] == slots[None, :, None]
    pick = jnp.where(chosen, 1.0, 0.0).reshape(n_experts * capacity, rows).astype(jnp.bfloat16)
    blend = jnp.where(chosen, weight.T[:, None, :], 0.0)
    blend = blend.reshape(n_experts * capacity, rows).astype(jnp.bfloat16)
    return pick, blend


def shards(
    queries,
    keys,
    values,
    resid,
    pair_ids,
    out_weight,
    norm_gain,
    experts,
    gates,
    w_gate,
    w_up,
    w_down,
):
    moe_rows = resid.shape[0]
    n_experts = lax.axis_size("seq") * w_gate.shape[0]
    capacity = 2 * moe_rows * TOP // n_experts
    core = lax.axis_index("exp")
    attended = attention(queries, keys, values, pair_ids)
    mine = lax.dynamic_slice_in_dim(attended, core * moe_rows, moe_rows, 0)
    yours = swap(lax.dynamic_slice_in_dim(attended, (1 - core) * moe_rows, moe_rows, 0))
    out_other = swap(out_weight)
    stream = (
        resid.astype(jnp.float32)
        + jnp.dot(mine, out_weight, preferred_element_type=jnp.float32)
        + jnp.dot(yours, out_other, preferred_element_type=jnp.float32)
    )
    meansq = jnp.mean(stream * stream, axis=-1, keepdims=True)
    normed = (stream * lax.rsqrt(meansq + 1e-05) * norm_gain).astype(jnp.bfloat16)
    pick, blend = routing(experts, gates, n_experts, capacity)
    outgoing = jnp.dot(pick, normed, preferred_element_type=jnp.float32).astype(jnp.bfloat16)
    width = normed.shape[1]
    cells = (SIDE, SIDE, SIDE, 3, capacity // 3, width)
    back = run_experts(outgoing.reshape(cells), w_gate[0].T, w_up[0].T, w_down[0])
    back = back.reshape(n_experts * capacity, width)
    mixture = lax.dot_general(
        blend, back, (((0,), (0,)), ((), ())), preferred_element_type=jnp.float32
    )
    return (stream + mixture).astype(jnp.bfloat16)


def solution(mesh):
    in_specs = (
        P("seq", "exp"),
        P("seq", "exp"),
        P("seq", "exp"),
        P(("seq", "exp"), None),
        P(),
        P("exp", None),
        P(),
        P(("seq", "exp"), None),
        P(("seq", "exp"), None),
        P("seq", None, "exp"),
        P("seq", None, "exp"),
        P("seq", "exp", None),
    )
    out_specs = P(("seq", "exp"), None)
    return jax.shard_map(shards, mesh=mesh, in_specs=in_specs, out_specs=out_specs, check_vma=False)
```

```python
import math

import jax
import jax.numpy as jnp
from jax import lax
from jax.experimental import pallas as pl
from jax.experimental.pallas import tpu as pltpu
from jax.sharding import PartitionSpec as P

HD = 128
TOP = 6
SWAP = [(0, 1), (1, 0)]
SIDE = 4
AXES = ("z", "y", "x")
SLICES = ((0, 640), (640, 640), (1280, 768))
FANS = ((2, 1, 0), (1, 0, 2), (0, 2, 1))
ORDERS = ((2, 1, 0), (1, 0, 2), (0, 2, 1))


def with_halo(cells, axis, dim, width):
    count = lax.axis_size(axis)
    ends = count - 1
    head = lax.slice_in_dim(cells, 0, width, axis=dim)
    tail = lax.slice_in_dim(cells, cells.shape[dim] - width, cells.shape[dim], axis=dim)
    return jnp.concatenate(
        [
            lax.ppermute(tail, axis, [(i, (i + 1) % count) for i in range(ends)]),
            cells,
            lax.ppermute(head, axis, [((i + 1) % count, i) for i in range(ends)]),
        ],
        axis=dim,
    )


def swap(block):
    return lax.ppermute(block, "exp", SWAP)


def peer(axis, delta):
    me = lax.axis_index("seq")
    at = [me // (SIDE * SIDE), (me // SIDE) % SIDE, me % SIDE]
    at[axis] = (at[axis] + delta) % SIDE
    return ((at[0] * SIDE + at[1]) * SIDE + at[2], lax.axis_index("exp"))


def cell(group, **fixed):
    return tuple(fixed.get(AXES[i], slice(None)) for i in range(3)) + (group,)


def tile(group, last, **fixed):
    c = ORDERS[group][2]
    rest = tuple(fixed.get(AXES[i], slice(None)) for i in range(3) if i != c)
    return (last, group) + rest


def spot(part, last, **fixed):
    rest = tuple(fixed.get(AXES[i], slice(None)) for i in range(3) if i != FANS[part][2])
    return (last,) + rest


def place(part, **fixed):
    start, width = SLICES[part]
    at = tuple(fixed.get(AXES[i], slice(None)) for i in range(3))
    return at + (slice(None), slice(None), pl.ds(start, width))


def picks(names, part):
    rows = names.shape[1]
    me = lax.axis_index("seq")
    here = [me // (SIDE * SIDE), (me // SIDE) % SIDE, me % SIDE]
    scale = (SIDE * SIDE, SIDE, 1)
    a, b, c = FANS[part]
    step = lax.broadcasted_iota(jnp.int32, (SIDE * SIDE, rows), 0)
    expert = (
        here[a] * scale[a]
        + (((step >> 2) + here[b]) & 3) * scale[b]
        + (((step & 3) + here[c]) & 3) * scale[c]
    ).astype(jnp.float32)
    named = jnp.zeros((SIDE * SIDE, rows), jnp.float32)
    for k in range(TOP):
        named += jnp.where(names[k : k + 1, :] == expert, 1.0, 0.0)
    earlier = lax.broadcasted_iota(jnp.int32, (rows, rows), 0)
    later = lax.broadcasted_iota(jnp.int32, (rows, rows), 1)
    before = jnp.where(earlier < later, 1.0, 0.0).astype(jnp.bfloat16)
    ranks = jnp.dot(named.astype(jnp.bfloat16), before, preferred_element_type=jnp.float32)
    ranks = jnp.where(named > 0.5, ranks, -1.0)
    slots = lax.broadcasted_iota(jnp.int32, (SIDE * SIDE, 24, rows), 1).astype(jnp.float32)
    pick = jnp.where(ranks[:, None, :] == slots, 1.0, 0.0)
    return pick.reshape(SIDE * SIDE * 24, rows).astype(jnp.bfloat16)


def expert_kernel(
    normed,
    names,
    gate_w,
    up_w,
    down_w,
    out,
    fan0,
    fan1,
    fan2,
    out0,
    out1,
    out2,
    mid0,
    mid1,
    mid2,
    far_names,
    arrived,
    result,
    third,
    fourth,
    weights,
    rows,
    act,
    local_sem,
    send_sem,
    recv_sem,
):
    mesh_id = pl.DeviceIdType.MESH
    partner = (lax.axis_index("seq"), 1 - lax.axis_index("exp"))
    barrier = pltpu.get_barrier_semaphore()
    for axis in range(3):
        for delta in range(1, SIDE):
            pl.semaphore_signal(barrier, inc=1, device_id=peer(axis, delta), device_id_type=mesh_id)
    pl.semaphore_signal(barrier, inc=1, device_id=partner, device_id_type=mesh_id)
    pl.semaphore_wait(barrier, 3 * (SIDE - 1) + 1)

    sent = []
    moved = []

    def send_to(device, source, target):
        copy = pltpu.make_async_remote_copy(
            src_ref=source,
            dst_ref=target,
            send_sem=send_sem.at[len(sent)],
            recv_sem=recv_sem.at[len(sent)],
            device_id=device,
            device_id_type=mesh_id,
        )
        copy.start()
        sent.append(copy)
        return copy

    def send(axis, delta, source, target):
        return send_to(peer(axis, delta), source, target)

    def move(source, target):
        copy = pltpu.make_async_copy(source, target, local_sem.at[len(moved)])
        copy.start()
        moved.append(copy)
        return copy

    groups = range(3)
    deltas = (2, 1, 3)
    inward = (1, 3, 2)
    name = [[AXES[axis] for axis in order] for order in ORDERS]
    fans, outs, mids = (fan0, fan1, fan2), (out0, out1, out2), (mid0, mid1, mid2)
    fan_name = [[AXES[axis] for axis in order] for order in FANS]
    one, two, three, info = {}, {}, [], {}
    for d in deltas:
        for f in groups:
            axis = FANS[f][0]
            info[f, d] = send(axis, d, names, far_names.at[f, SIDE - d])
            one[f, d] = send(
                axis, d, normed.at[:, pl.ds(*SLICES[f])], fans[f].at[SIDE - d]
            )
    swapped = []
    own = []
    for i, w in enumerate((gate_w, up_w, down_w)):
        swapped.append(send_to(partner, w, weights.at[1, i]))
        own.append(move(w, weights.at[0, i]))

    def select(f, r):
        start, wide = SLICES[f]
        _, nb, _ = fan_name[f]
        na = fan_name[f][0]
        table = names[...] if r == 0 else far_names[f, r]
        tokens = normed[:, start : start + wide] if r == 0 else fans[f][r]
        chosen = jnp.dot(picks(table, f), tokens, preferred_element_type=jnp.float32)
        chosen = chosen.reshape(SIDE, SIDE, 3, 8, wide)
        mids[f][spot(f, slice(None), **{na: r, nb: 0})] = chosen[0].astype(jnp.bfloat16)
        for d in range(1, SIDE):
            outs[f][d, :, r] = chosen[d].astype(jnp.bfloat16)

    for r in (0,) + inward:
        for f in groups:
            na, nb, _ = fan_name[f]
            if r:
                info[f, SIDE - r].wait_recv()
                one[f, SIDE - r].wait_recv()
            select(f, r)
            for d in deltas:
                two[f, r, d] = send(
                    FANS[f][1],
                    d,
                    outs[f].at[d, :, r],
                    mids[f].at[spot(f, slice(None), **{na: r, nb: SIDE - d})],
                )
    kept = []
    for i in (0,) + inward:
        for f in groups:
            _, nb, nc = fan_name[f]
            if i:
                for r in range(SIDE):
                    two[f, r, SIDE - i].wait_recv()
            for d in deltas:
                three.append(
                    send(
                        FANS[f][2],
                        d,
                        mids[f].at[spot(f, d, **{nb: i})],
                        arrived.at[place(f, **{nb: i, nc: SIDE - d})],
                    )
                )
            kept.append(
                move(mids[f].at[spot(f, 0, **{nb: i})], arrived.at[place(f, **{nb: i, nc: 0})])
            )
    for copy in three:
        copy.wait_recv()
    for copy in swapped:
        copy.wait_recv()
    for copy in own + kept:
        copy.wait()

    batch = rows.shape[0]
    width = rows.shape[1]
    chunk = 512
    contract = (((1,), (1,)), ((), ()))

    def ffn(j):
        part = batch // 3
        for g in groups:
            block = arrived[cell(g, **{name[g][2]: j})].astype(jnp.float32)
            rows[g * part : (g + 1) * part, :] = block.reshape(part, width).astype(jnp.bfloat16)

        @pl.loop(0, 2)
        def _(h):
            gate = lax.dot_general(
                rows[...], weights[h, 0], contract, preferred_element_type=jnp.float32
            )
            up = lax.dot_general(
                rows[...], weights[h, 1], contract, preferred_element_type=jnp.float32
            )
            act[h] = (gate / (1.0 + jnp.exp(-gate)) * up).astype(jnp.bfloat16)

        for n in range(0, width, chunk):
            cols = slice(n, n + chunk)
            total = jnp.dot(act[0], weights[0, 2, :, cols], preferred_element_type=jnp.float32)
            total += jnp.dot(act[1], weights[1, 2, :, cols], preferred_element_type=jnp.float32)
            total = total.reshape(result.shape[1:5] + (chunk,))
            result[j, :, :, :, :, cols] = total.astype(jnp.bfloat16)

    back_one, back_two, back_three = {}, {}, []

    def back_relay(j, g):
        held = result if j == 0 else third
        nb = name[g][1]
        for d in deltas:
            back_two[g, j, d] = send(
                ORDERS[g][1],
                d,
                held.at[tile(g, j, **{nb: d})],
                fourth.at[tile(g, j, **{nb: SIDE - d})],
            )

    def back_direct(j, g):
        held = result if j == 0 else third
        na, nb, nc = name[g]
        for d in deltas:
            back_three.append(
                send(
                    ORDERS[g][0],
                    d,
                    held.at[tile(g, j, **{na: d, nb: 0})],
                    out.at[cell(g, **{na: SIDE - d, nb: 0, nc: j})],
                )
            )
        move(held.at[tile(g, j, **{na: 0, nb: 0})], out.at[cell(g, **{na: 0, nb: 0, nc: j})])

    for j in (0,) + inward:
        ffn(j)
        for g in groups:
            if j:
                back_one[g, j] = send(
                    ORDERS[g][2], j, result.at[tile(g, j)], third.at[tile(g, SIDE - j)]
                )
            else:
                back_relay(0, g)
    for g in groups:
        back_direct(0, g)
    for j in (3, 1, 2):
        for g in groups:
            back_one[g, SIDE - j].wait_recv()
            back_relay(j, g)
        for g in groups:
            back_direct(j, g)
    for b in inward:
        for g in groups:
            for j in range(SIDE):
                back_two[g, j, SIDE - b].wait_recv()
        for g in groups:
            na, nb, _ = name[g]
            for d in deltas:
                back_three.append(
                    send(
                        ORDERS[g][0],
                        d,
                        fourth.at[tile(g, slice(None), **{na: d, nb: b})],
                        out.at[cell(g, **{na: SIDE - d, nb: b})],
                    )
                )
            move(
                fourth.at[tile(g, slice(None), **{na: 0, nb: b})],
                out.at[cell(g, **{na: 0, nb: b})],
            )
    for copy in back_three:
        copy.wait_recv()
    for copy in moved[len(own) + len(kept) :]:
        copy.wait()
    for copy in sent:
        copy.wait_send()


def run_experts(normed, names, gate_w, up_w, down_w):
    dtype = normed.dtype
    tokens = normed.shape[0]
    hidden, width = down_w.shape
    cells = (SIDE, SIDE, SIDE, 3, 8)
    by_last = (SIDE, 3, SIDE, SIDE, 8, width)
    batch = 3 * SIDE * SIDE * 8
    copies = 3 * (2 * 3 + 4 * 3 + 4 * 3) + 3 + 3 * (3 + 4 * 3 + 3 * (4 + 3))
    vmem = pl.BlockSpec(memory_space=pltpu.VMEM)
    hbm = pl.BlockSpec(memory_space=pl.ANY)
    return pl.pallas_call(
        expert_kernel,
        out_shape=jax.ShapeDtypeStruct(cells + (width,), dtype),
        in_specs=[vmem, vmem, hbm, hbm, hbm],
        out_specs=hbm,
        scratch_shapes=[pltpu.VMEM((SIDE, tokens, wide), dtype) for _, wide in SLICES]
        + [pltpu.VMEM(cells + (wide,), dtype) for _, wide in SLICES]
        + [pltpu.VMEM(cells + (wide,), dtype) for _, wide in SLICES]
        + [
            pltpu.VMEM((3, SIDE, 8, tokens), jnp.float32),
            pltpu.VMEM(cells + (width,), dtype),
            pltpu.VMEM(by_last, dtype),
            pltpu.VMEM(by_last, dtype),
            pltpu.VMEM(by_last, dtype),
            pltpu.VMEM((2, 3, hidden, width), dtype),
            pltpu.VMEM((batch, width), dtype),
            pltpu.VMEM((2, batch, hidden), dtype),
            pltpu.SemaphoreType.DMA((3 + 3 * 4 + 3 * (4 + 3),)),
            pltpu.SemaphoreType.DMA((copies,)),
            pltpu.SemaphoreType.DMA((copies,)),
        ],
        compiler_params=pltpu.CompilerParams(
            collective_id=0, has_side_effects=True, vmem_limit_bytes=60 << 20
        ),
        name="run_experts",
    )(normed, names, gate_w, up_w, down_w)


def attention(queries, keys, values, pair_ids):
    tok_rows, local_width = queries.shape
    local_heads = local_width // HD
    shard = lax.axis_index("seq")
    widened = with_halo(jnp.stack([keys, values]), "seq", 1, tok_rows)
    id_pad = jnp.pad(pair_ids, (tok_rows, tok_rows), constant_values=-1)
    key_ids = lax.dynamic_slice_in_dim(id_pad, shard * tok_rows, 3 * tok_rows, 0)
    query_ids = lax.dynamic_slice_in_dim(id_pad, shard * tok_rows + tok_rows, tok_rows, 0)
    query_pos = jnp.arange(tok_rows, dtype=jnp.int32) + tok_rows
    key_pos = jnp.arange(3 * tok_rows, dtype=jnp.int32)
    allowed = (query_ids[:, None] == key_ids[None, :]) & (
        jnp.abs(query_pos[:, None] - key_pos[None, :]) < tok_rows
    )
    query_heads = queries.reshape(tok_rows, local_heads, HD)
    key_heads = widened[0].reshape(3 * tok_rows, local_heads, HD)
    value_heads = widened[1].reshape(3 * tok_rows, local_heads, HD)
    score = jnp.einsum(
        "qhd,khd->hqk", query_heads, key_heads, preferred_element_type=jnp.float32
    ) / math.sqrt(HD)
    score = jnp.where(allowed[None], score, -jnp.inf)
    top = jnp.max(score, axis=-1, keepdims=True)
    weights = jnp.exp(score - top)
    probs = (weights / jnp.sum(weights, axis=-1, keepdims=True)).astype(jnp.bfloat16)
    attended = jnp.einsum("hqk,khd->qhd", probs, value_heads, preferred_element_type=jnp.float32)
    return attended.reshape(tok_rows, local_width).astype(jnp.bfloat16)


def routing(experts, gates, n_experts, capacity):
    rows = experts.shape[0]
    step = jnp.arange(n_experts, dtype=jnp.int32)
    me = lax.axis_index("seq")
    names = (
        (step // 16 + me // 16) % SIDE * 16
        + (step // 4 % SIDE + me // 4 % SIDE) % SIDE * 4
        + (step % SIDE + me % SIDE) % SIDE
    )
    hits = experts[:, :, None] == names[None, None, :]
    named = jnp.sum(hits.astype(jnp.float32), axis=1)
    weight = jnp.sum(jnp.where(hits, gates[:, :, None], 0.0), axis=1)
    order = jnp.arange(rows, dtype=jnp.int32)
    before = (order[None, :] < order[:, None]).astype(jnp.bfloat16)
    ranks = jnp.dot(before, named.astype(jnp.bfloat16), preferred_element_type=jnp.float32)
    ranks = jnp.where(named > 0.0, ranks, -1.0)
    slots = jnp.arange(capacity, dtype=jnp.int32).astype(jnp.float32)
    chosen = ranks.T[:, None, :] == slots[None, :, None]
    blend = jnp.where(chosen, weight.T[:, None, :], 0.0)
    blend = blend.reshape(n_experts * capacity, rows).astype(jnp.bfloat16)
    return blend


def shards(
    queries,
    keys,
    values,
    resid,
    pair_ids,
    out_weight,
    norm_gain,
    experts,
    gates,
    w_gate,
    w_up,
    w_down,
):
    moe_rows = resid.shape[0]
    n_experts = lax.axis_size("seq") * w_gate.shape[0]
    capacity = 2 * moe_rows * TOP // n_experts
    core = lax.axis_index("exp")
    attended = attention(queries, keys, values, pair_ids)
    mine = lax.dynamic_slice_in_dim(attended, core * moe_rows, moe_rows, 0)
    yours = swap(lax.dynamic_slice_in_dim(attended, (1 - core) * moe_rows, moe_rows, 0))
    out_other = swap(out_weight)
    stream = (
        resid.astype(jnp.float32)
        + jnp.dot(mine, out_weight, preferred_element_type=jnp.float32)
        + jnp.dot(yours, out_other, preferred_element_type=jnp.float32)
    )
    meansq = jnp.mean(stream * stream, axis=-1, keepdims=True)
    normed = (stream * lax.rsqrt(meansq + 1e-05) * norm_gain).astype(jnp.bfloat16)
    blend = routing(experts, gates, n_experts, capacity)
    width = normed.shape[1]
    names = jnp.pad(experts.T.astype(jnp.float32), ((0, 8 - TOP), (0, 0)), constant_values=-1.0)
    back = run_experts(normed, names, w_gate[0].T, w_up[0].T, w_down[0])
    back = back.reshape(n_experts * capacity, width)
    mixture = lax.dot_general(
        blend, back, (((0,), (0,)), ((), ())), preferred_element_type=jnp.float32
    )
    return (stream + mixture).astype(jnp.bfloat16)


def solution(mesh):
    in_specs = (
        P("seq", "exp"),
        P("seq", "exp"),
        P("seq", "exp"),
        P(("seq", "exp"), None),
        P(),
        P("exp", None),
        P(),
        P(("seq", "exp"), None),
        P(("seq", "exp"), None),
        P("seq", None, "exp"),
        P("seq", None, "exp"),
        P("seq", "exp", None),
    )
    out_specs = P(("seq", "exp"), None)
    return jax.shard_map(shards, mesh=mesh, in_specs=in_specs, out_specs=out_specs, check_vma=False)
```

```python
import math

import jax
import jax.numpy as jnp
from jax import lax
from jax.experimental import pallas as pl
from jax.experimental.pallas import tpu as pltpu
from jax.sharding import PartitionSpec as P

HD = 128
TOP = 6
SWAP = [(0, 1), (1, 0)]
SIDE = 4
AXES = ("z", "y", "x")
SLICES = ((0, 640), (640, 640), (1280, 768))
FANS = ((2, 1, 0), (1, 0, 2), (0, 2, 1))


def with_halo(cells, axis, dim, width):
    count = lax.axis_size(axis)
    ends = count - 1
    head = lax.slice_in_dim(cells, 0, width, axis=dim)
    tail = lax.slice_in_dim(cells, cells.shape[dim] - width, cells.shape[dim], axis=dim)
    return jnp.concatenate(
        [
            lax.ppermute(tail, axis, [(i, (i + 1) % count) for i in range(ends)]),
            cells,
            lax.ppermute(head, axis, [((i + 1) % count, i) for i in range(ends)]),
        ],
        axis=dim,
    )


def swap(block):
    return lax.ppermute(block, "exp", SWAP)


def peer(axis, delta):
    me = lax.axis_index("seq")
    at = [me // (SIDE * SIDE), (me // SIDE) % SIDE, me % SIDE]
    at[axis] = (at[axis] + delta) % SIDE
    return ((at[0] * SIDE + at[1]) * SIDE + at[2], lax.axis_index("exp"))


def spot(part, last, **fixed):
    rest = tuple(fixed.get(AXES[i], slice(None)) for i in range(3) if i != FANS[part][2])
    return (last,) + rest


def place(part, **fixed):
    start, width = SLICES[part]
    at = tuple(fixed.get(AXES[i], slice(None)) for i in range(3))
    return at + (slice(None), slice(None), pl.ds(start, width))


def picks(names, part, blend=False):
    rows = names.shape[1]
    me = lax.axis_index("seq")
    here = [me // (SIDE * SIDE), (me // SIDE) % SIDE, me % SIDE]
    scale = (SIDE * SIDE, SIDE, 1)
    a, b, c = FANS[part]
    step = lax.broadcasted_iota(jnp.int32, (SIDE * SIDE, rows), 0)
    expert = (
        here[a] * scale[a]
        + (((step >> 2) + here[b]) & 3) * scale[b]
        + (((step & 3) + here[c]) & 3) * scale[c]
    ).astype(jnp.float32)
    named = jnp.zeros((SIDE * SIDE, rows), jnp.float32)
    weight = jnp.zeros((SIDE * SIDE, rows), jnp.float32)
    for k in range(TOP):
        hit = names[k : k + 1, :] == expert
        named += jnp.where(hit, 1.0, 0.0)
        weight += jnp.where(hit, names[8 + k : 9 + k, :], 0.0)
    earlier = lax.broadcasted_iota(jnp.int32, (rows, rows), 0)
    later = lax.broadcasted_iota(jnp.int32, (rows, rows), 1)
    before = jnp.where(earlier < later, 1.0, 0.0).astype(jnp.bfloat16)
    ranks = jnp.dot(named.astype(jnp.bfloat16), before, preferred_element_type=jnp.float32)
    ranks = jnp.where(named > 0.5, ranks, -1.0)
    slots = lax.broadcasted_iota(jnp.int32, (SIDE * SIDE, 24, rows), 1).astype(jnp.float32)
    chosen = ranks[:, None, :] == slots
    pick = jnp.where(chosen, weight[:, None, :] if blend else 1.0, 0.0)
    return pick.reshape(SIDE * SIDE * 24, rows).astype(jnp.bfloat16)


def expert_kernel(
    normed,
    names,
    stream,
    gate_w,
    up_w,
    down_w,
    out,
    fan0,
    fan1,
    fan2,
    out0,
    out1,
    out2,
    mid0,
    mid1,
    mid2,
    far_names,
    arrived,
    result,
    ret0,
    ret1,
    ret2,
    home0,
    home1,
    home2,
    part0,
    part1,
    part2,
    got0,
    got1,
    got2,
    weights,
    rows,
    act,
    local_sem,
    send_sem,
    recv_sem,
):
    mesh_id = pl.DeviceIdType.MESH
    partner = (lax.axis_index("seq"), 1 - lax.axis_index("exp"))
    barrier = pltpu.get_barrier_semaphore()
    for axis in range(3):
        for delta in range(1, SIDE):
            pl.semaphore_signal(barrier, inc=1, device_id=peer(axis, delta), device_id_type=mesh_id)
    pl.semaphore_signal(barrier, inc=1, device_id=partner, device_id_type=mesh_id)
    pl.semaphore_wait(barrier, 3 * (SIDE - 1) + 1)

    sent = []
    moved = []

    def send_to(device, source, target):
        copy = pltpu.make_async_remote_copy(
            src_ref=source,
            dst_ref=target,
            send_sem=send_sem.at[len(sent)],
            recv_sem=recv_sem.at[len(sent)],
            device_id=device,
            device_id_type=mesh_id,
        )
        copy.start()
        sent.append(copy)
        return copy

    def send(axis, delta, source, target):
        return send_to(peer(axis, delta), source, target)

    def move(source, target):
        copy = pltpu.make_async_copy(source, target, local_sem.at[len(moved)])
        copy.start()
        moved.append(copy)
        return copy

    groups = range(3)
    deltas = (2, 1, 3)
    inward = (1, 3, 2)
    fans, outs, mids = (fan0, fan1, fan2), (out0, out1, out2), (mid0, mid1, mid2)
    fan_name = [[AXES[axis] for axis in order] for order in FANS]
    one, two, three, info = {}, {}, [], {}
    for d in deltas:
        for f in groups:
            axis = FANS[f][0]
            info[f, d] = send(axis, d, names, far_names.at[f, SIDE - d])
            one[f, d] = send(
                axis, d, normed.at[:, pl.ds(*SLICES[f])], fans[f].at[SIDE - d]
            )
    swapped = []
    own = []
    for i, w in enumerate((gate_w, up_w, down_w)):
        swapped.append(send_to(partner, w, weights.at[1, i]))
        own.append(move(w, weights.at[0, i]))

    def select(f, r):
        start, wide = SLICES[f]
        _, nb, _ = fan_name[f]
        na = fan_name[f][0]
        table = names[...] if r == 0 else far_names[f, r]
        tokens = normed[:, start : start + wide] if r == 0 else fans[f][r]
        chosen = jnp.dot(picks(table, f), tokens, preferred_element_type=jnp.float32)
        chosen = chosen.reshape(SIDE, SIDE, 3, 8, wide)
        mids[f][spot(f, slice(None), **{na: r, nb: 0})] = chosen[0].astype(jnp.bfloat16)
        for d in range(1, SIDE):
            outs[f][d, :, r] = chosen[d].astype(jnp.bfloat16)

    for r in (0,) + inward:
        for f in groups:
            na, nb, _ = fan_name[f]
            if r:
                info[f, SIDE - r].wait_recv()
                one[f, SIDE - r].wait_recv()
            select(f, r)
            for d in deltas:
                two[f, r, d] = send(
                    FANS[f][1],
                    d,
                    outs[f].at[d, :, r],
                    mids[f].at[spot(f, slice(None), **{na: r, nb: SIDE - d})],
                )
    kept = []
    for i in (0,) + inward:
        for f in groups:
            _, nb, nc = fan_name[f]
            if i:
                for r in range(SIDE):
                    two[f, r, SIDE - i].wait_recv()
            for d in deltas:
                three.append(
                    send(
                        FANS[f][2],
                        d,
                        mids[f].at[spot(f, d, **{nb: i})],
                        arrived.at[place(f, **{nb: i, nc: SIDE - d})],
                    )
                )
            kept.append(
                move(mids[f].at[spot(f, 0, **{nb: i})], arrived.at[place(f, **{nb: i, nc: 0})])
            )
    for copy in three:
        copy.wait_recv()
    for copy in swapped:
        copy.wait_recv()
    for copy in own + kept:
        copy.wait()

    batch = rows.shape[0]
    width = rows.shape[1]
    chunk = 512
    contract = (((1,), (1,)), ((), ()))

    def ffn(j):
        rows[...] = arrived[j].astype(jnp.float32).reshape(batch, width).astype(jnp.bfloat16)

        @pl.loop(0, 2)
        def _(h):
            gate = lax.dot_general(
                rows[...], weights[h, 0], contract, preferred_element_type=jnp.float32
            )
            up = lax.dot_general(
                rows[...], weights[h, 1], contract, preferred_element_type=jnp.float32
            )
            act[h] = (gate / (1.0 + jnp.exp(-gate)) * up).astype(jnp.bfloat16)

        for n in range(0, width, chunk):
            cols = slice(n, n + chunk)
            total = jnp.dot(act[0], weights[0, 2, :, cols], preferred_element_type=jnp.float32)
            total += jnp.dot(act[1], weights[1, 2, :, cols], preferred_element_type=jnp.float32)
            total = total.reshape(result.shape[1:5] + (chunk,))
            result[j, :, :, :, :, cols] = total.astype(jnp.bfloat16)

    rets, homes = (ret0, ret1, ret2), (home0, home1, home2)
    parts, gots = (part0, part1, part2), (got0, got1, got2)
    back_one, back_two, back_three, stay, home = {}, {}, {}, {}, {}
    for j in (0,) + inward:
        ffn(j)
        for f in groups:
            axis = FANS[f][2]
            for d in (0,) + deltas:
                at = {"z": j}
                if axis == 0 and d != j:
                    continue
                if axis:
                    at[AXES[axis]] = d
                rest = {} if axis == 0 else {"z": j}
                source = result.at[place(f, **at)]
                if d:
                    back_one.setdefault((f, SIDE - d), []).append(
                        send(axis, d, source, rets[f].at[spot(f, SIDE - d, **rest)])
                    )
                else:
                    stay.setdefault(f, []).append(
                        move(source, rets[f].at[spot(f, 0, **rest)])
                    )
    for j in (0,) + inward:
        for f in groups:
            nb = fan_name[f][1]
            if j:
                for copy in back_one[f, j]:
                    copy.wait_recv()
            else:
                for copy in stay[f]:
                    copy.wait()
            for d in deltas:
                back_two.setdefault((f, SIDE - d), []).append(
                    send(
                        FANS[f][1],
                        d,
                        rets[f].at[spot(f, j, **{nb: d})],
                        homes[f].at[SIDE - d, j],
                    )
                )
            home.setdefault(f, []).append(
                move(rets[f].at[spot(f, j, **{nb: 0})], homes[f].at[0, j])
            )

    def blended(f, r):
        wide = SLICES[f][1]
        table = names[...] if r == 0 else far_names[f, r]
        held = homes[f][:, :, r].astype(jnp.float32)
        held = held.reshape(SIDE * SIDE * 24, wide).astype(jnp.bfloat16)
        return lax.dot_general(
            picks(table, f, True),
            held,
            (((0,), (0,)), ((), ())),
            preferred_element_type=jnp.float32,
        )

    for f in groups:
        for i in range(1, SIDE):
            for copy in back_two[f, i]:
                copy.wait_recv()
        for copy in home[f]:
            copy.wait()
        for r in deltas:
            parts[f][r] = blended(f, r).astype(jnp.bfloat16)
        for r in deltas:
            back_three[f, SIDE - r] = send(
                FANS[f][0], r, parts[f].at[r], gots[f].at[SIDE - r]
            )
    for f in groups:
        start, wide = SLICES[f]
        total = stream[:, start : start + wide] + blended(f, 0)
        for r in range(1, SIDE):
            back_three[f, r].wait_recv()
            total += gots[f][r].astype(jnp.float32)
        out[:, start : start + wide] = total.astype(out.dtype)
    for copy in sent:
        copy.wait_send()


def run_experts(normed, names, stream, gate_w, up_w, down_w):
    dtype = normed.dtype
    tokens = normed.shape[0]
    hidden, width = down_w.shape
    cells = (SIDE, SIDE, SIDE, 3, 8)
    batch = 3 * SIDE * SIDE * 8
    copies = 3 * (2 * 3 + 4 * 3 + 4 * 3) + 3 + (3 + 2 * 4 * 3) + 3 * (4 * 3 + 3)
    vmem = pl.BlockSpec(memory_space=pltpu.VMEM)
    hbm = pl.BlockSpec(memory_space=pl.ANY)
    return pl.pallas_call(
        expert_kernel,
        out_shape=jax.ShapeDtypeStruct((tokens, width), dtype),
        in_specs=[vmem, vmem, vmem, hbm, hbm, hbm],
        out_specs=vmem,
        scratch_shapes=[pltpu.VMEM((SIDE, tokens, wide), dtype) for _, wide in SLICES]
        + [pltpu.VMEM(cells + (wide,), dtype) for _, wide in SLICES]
        + [pltpu.VMEM(cells + (wide,), dtype) for _, wide in SLICES]
        + [
            pltpu.VMEM((3, SIDE, 16, tokens), jnp.float32),
            pltpu.VMEM(cells + (width,), dtype),
            pltpu.VMEM(cells + (width,), dtype),
        ]
        + [pltpu.VMEM(cells + (wide,), dtype) for _, wide in SLICES]
        + [pltpu.VMEM(cells + (wide,), dtype) for _, wide in SLICES]
        + [pltpu.VMEM((SIDE, tokens, wide), dtype) for _, wide in SLICES]
        + [pltpu.VMEM((SIDE, tokens, wide), dtype) for _, wide in SLICES]
        + [
            pltpu.VMEM((2, 3, hidden, width), dtype),
            pltpu.VMEM((batch, width), dtype),
            pltpu.VMEM((2, batch, hidden), dtype),
            pltpu.SemaphoreType.DMA((3 + 3 * 4 + (1 + 2 * 4) + 3 * 4,)),
            pltpu.SemaphoreType.DMA((copies,)),
            pltpu.SemaphoreType.DMA((copies,)),
        ],
        compiler_params=pltpu.CompilerParams(
            collective_id=0, has_side_effects=True, vmem_limit_bytes=60 << 20
        ),
        name="run_experts",
    )(normed, names, stream, gate_w, up_w, down_w)


def attention(queries, keys, values, pair_ids):
    tok_rows, local_width = queries.shape
    local_heads = local_width // HD
    shard = lax.axis_index("seq")
    widened = with_halo(jnp.stack([keys, values]), "seq", 1, tok_rows)
    id_pad = jnp.pad(pair_ids, (tok_rows, tok_rows), constant_values=-1)
    key_ids = lax.dynamic_slice_in_dim(id_pad, shard * tok_rows, 3 * tok_rows, 0)
    query_ids = lax.dynamic_slice_in_dim(id_pad, shard * tok_rows + tok_rows, tok_rows, 0)
    query_pos = jnp.arange(tok_rows, dtype=jnp.int32) + tok_rows
    key_pos = jnp.arange(3 * tok_rows, dtype=jnp.int32)
    allowed = (query_ids[:, None] == key_ids[None, :]) & (
        jnp.abs(query_pos[:, None] - key_pos[None, :]) < tok_rows
    )
    query_heads = queries.reshape(tok_rows, local_heads, HD)
    key_heads = widened[0].reshape(3 * tok_rows, local_heads, HD)
    value_heads = widened[1].reshape(3 * tok_rows, local_heads, HD)
    score = jnp.einsum(
        "qhd,khd->hqk", query_heads, key_heads, preferred_element_type=jnp.float32
    ) / math.sqrt(HD)
    score = jnp.where(allowed[None], score, -jnp.inf)
    top = jnp.max(score, axis=-1, keepdims=True)
    weights = jnp.exp(score - top)
    probs = (weights / jnp.sum(weights, axis=-1, keepdims=True)).astype(jnp.bfloat16)
    attended = jnp.einsum("hqk,khd->qhd", probs, value_heads, preferred_element_type=jnp.float32)
    return attended.reshape(tok_rows, local_width).astype(jnp.bfloat16)


def shards(
    queries,
    keys,
    values,
    resid,
    pair_ids,
    out_weight,
    norm_gain,
    experts,
    gates,
    w_gate,
    w_up,
    w_down,
):
    moe_rows = resid.shape[0]
    core = lax.axis_index("exp")
    attended = attention(queries, keys, values, pair_ids)
    mine = lax.dynamic_slice_in_dim(attended, core * moe_rows, moe_rows, 0)
    yours = swap(lax.dynamic_slice_in_dim(attended, (1 - core) * moe_rows, moe_rows, 0))
    out_other = swap(out_weight)
    stream = (
        resid.astype(jnp.float32)
        + jnp.dot(mine, out_weight, preferred_element_type=jnp.float32)
        + jnp.dot(yours, out_other, preferred_element_type=jnp.float32)
    )
    meansq = jnp.mean(stream * stream, axis=-1, keepdims=True)
    normed = (stream * lax.rsqrt(meansq + 1e-05) * norm_gain).astype(jnp.bfloat16)
    lines = ((0, 8 - TOP), (0, 0))
    names = jnp.concatenate(
        [
            jnp.pad(experts.T.astype(jnp.float32), lines, constant_values=-1.0),
            jnp.pad(gates.T, lines),
        ]
    )
    return run_experts(normed, names, stream, w_gate[0].T, w_up[0].T, w_down[0])


def solution(mesh):
    in_specs = (
        P("seq", "exp"),
        P("seq", "exp"),
        P("seq", "exp"),
        P(("seq", "exp"), None),
        P(),
        P("exp", None),
        P(),
        P(("seq", "exp"), None),
        P(("seq", "exp"), None),
        P("seq", None, "exp"),
        P("seq", None, "exp"),
        P("seq", "exp", None),
    )
    out_specs = P(("seq", "exp"), None)
    return jax.shard_map(shards, mesh=mesh, in_specs=in_specs, out_specs=out_specs, check_vma=False)
```

```python
import math

import jax
import jax.numpy as jnp
from jax import lax
from jax.experimental import pallas as pl
from jax.experimental.pallas import tpu as pltpu
from jax.sharding import PartitionSpec as P

HD = 128
TOP = 6
SWAP = [(0, 1), (1, 0)]
SIDE = 4
AXES = ("z", "y", "x")
SLICES = ((0, 640), (640, 640), (1280, 768))
FANS = ((2, 1, 0), (1, 0, 2), (0, 2, 1))


def with_halo(cells, axis, dim, width):
    count = lax.axis_size(axis)
    ends = count - 1
    head = lax.slice_in_dim(cells, 0, width, axis=dim)
    tail = lax.slice_in_dim(cells, cells.shape[dim] - width, cells.shape[dim], axis=dim)
    return jnp.concatenate(
        [
            lax.ppermute(tail, axis, [(i, (i + 1) % count) for i in range(ends)]),
            cells,
            lax.ppermute(head, axis, [((i + 1) % count, i) for i in range(ends)]),
        ],
        axis=dim,
    )


def swap(block):
    return lax.ppermute(block, "exp", SWAP)


def peer(axis, delta):
    me = lax.axis_index("seq")
    at = [me // (SIDE * SIDE), (me // SIDE) % SIDE, me % SIDE]
    at[axis] = (at[axis] + delta) % SIDE
    return ((at[0] * SIDE + at[1]) * SIDE + at[2], lax.axis_index("exp"))


def spot(part, last, **fixed):
    rest = tuple(fixed.get(AXES[i], slice(None)) for i in range(3) if i != FANS[part][2])
    return (last,) + rest


def place(part, **fixed):
    start, width = SLICES[part]
    at = tuple(fixed.get(AXES[i], slice(None)) for i in range(3))
    return at + (slice(None), slice(None), pl.ds(start, width))


def picks(names, part, blend=False):
    rows = names.shape[1]
    me = lax.axis_index("seq")
    here = [me // (SIDE * SIDE), (me // SIDE) % SIDE, me % SIDE]
    scale = (SIDE * SIDE, SIDE, 1)
    a, b, c = FANS[part]
    step = lax.broadcasted_iota(jnp.int32, (SIDE * SIDE, rows), 0)
    expert = (
        here[a] * scale[a]
        + (((step >> 2) + here[b]) & 3) * scale[b]
        + (((step & 3) + here[c]) & 3) * scale[c]
    ).astype(jnp.float32)
    named = jnp.zeros((SIDE * SIDE, rows), jnp.float32)
    weight = jnp.zeros((SIDE * SIDE, rows), jnp.float32)
    for k in range(TOP):
        hit = names[k : k + 1, :] == expert
        named += jnp.where(hit, 1.0, 0.0)
        weight += jnp.where(hit, names[8 + k : 9 + k, :], 0.0)
    earlier = lax.broadcasted_iota(jnp.int32, (rows, rows), 0)
    later = lax.broadcasted_iota(jnp.int32, (rows, rows), 1)
    before = jnp.where(earlier < later, 1.0, 0.0).astype(jnp.bfloat16)
    ranks = jnp.dot(named.astype(jnp.bfloat16), before, preferred_element_type=jnp.float32)
    ranks = jnp.where(named > 0.5, ranks, -1.0)
    slots = lax.broadcasted_iota(jnp.int32, (SIDE * SIDE, 24, rows), 1).astype(jnp.float32)
    chosen = ranks[:, None, :] == slots
    pick = jnp.where(chosen, weight[:, None, :] if blend else 1.0, 0.0)
    return pick.reshape(SIDE * SIDE * 24, rows).astype(jnp.bfloat16)


def expert_kernel(
    normed,
    names,
    stream,
    gate_w,
    up_w,
    down_w,
    out,
    fan0,
    fan1,
    fan2,
    out0,
    out1,
    out2,
    mid0,
    mid1,
    mid2,
    far_names,
    arrived,
    result,
    ret0,
    ret1,
    ret2,
    home0,
    home1,
    home2,
    part0,
    part1,
    part2,
    got0,
    got1,
    got2,
    weights,
    rows,
    act,
    local_sem,
    send_sem,
    recv_sem,
):
    mesh_id = pl.DeviceIdType.MESH
    partner = (lax.axis_index("seq"), 1 - lax.axis_index("exp"))
    barrier = pltpu.get_barrier_semaphore()
    for axis in range(3):
        for delta in range(1, SIDE):
            pl.semaphore_signal(barrier, inc=1, device_id=peer(axis, delta), device_id_type=mesh_id)
    pl.semaphore_signal(barrier, inc=1, device_id=partner, device_id_type=mesh_id)
    pl.semaphore_wait(barrier, 3 * (SIDE - 1) + 1)

    sent = []
    moved = []

    def send_to(device, source, target):
        copy = pltpu.make_async_remote_copy(
            src_ref=source,
            dst_ref=target,
            send_sem=send_sem.at[len(sent)],
            recv_sem=recv_sem.at[len(sent)],
            device_id=device,
            device_id_type=mesh_id,
        )
        copy.start()
        sent.append(copy)
        return copy

    def send(axis, delta, source, target):
        return send_to(peer(axis, delta), source, target)

    def move(source, target):
        copy = pltpu.make_async_copy(source, target, local_sem.at[len(moved)])
        copy.start()
        moved.append(copy)
        return copy

    groups = range(3)
    deltas = (2, 1, 3)
    inward = (1, 3, 2)
    fans, outs, mids = (fan0, fan1, fan2), (out0, out1, out2), (mid0, mid1, mid2)
    fan_name = [[AXES[axis] for axis in order] for order in FANS]
    one, two, three, info = {}, {}, [], {}
    for d in deltas:
        for f in groups:
            axis = FANS[f][0]
            info[f, d] = send(axis, d, names, far_names.at[f, SIDE - d])
            one[f, d] = send(
                axis, d, normed.at[:, pl.ds(*SLICES[f])], fans[f].at[SIDE - d]
            )
    swapped = []
    own = []
    for i, w in enumerate((gate_w, up_w, down_w)):
        swapped.append(send_to(partner, w, weights.at[1, i]))
        own.append(move(w, weights.at[0, i]))

    def select(f, r):
        start, wide = SLICES[f]
        _, nb, _ = fan_name[f]
        na = fan_name[f][0]
        table = names[...] if r == 0 else far_names[f, r]
        tokens = normed[:, start : start + wide] if r == 0 else fans[f][r]
        chosen = jnp.dot(picks(table, f), tokens, preferred_element_type=jnp.float32)
        chosen = chosen.reshape(SIDE, SIDE, 3, 8, wide)
        mids[f][spot(f, slice(None), **{na: r, nb: 0})] = chosen[0].astype(jnp.bfloat16)
        for d in range(1, SIDE):
            outs[f][d, :, r] = chosen[d].astype(jnp.bfloat16)

    for r in (0,) + inward:
        for f in groups:
            na, nb, _ = fan_name[f]
            if r:
                info[f, SIDE - r].wait_recv()
                one[f, SIDE - r].wait_recv()
            select(f, r)
            for d in deltas:
                two[f, r, d] = send(
                    FANS[f][1],
                    d,
                    outs[f].at[d, :, r],
                    mids[f].at[spot(f, slice(None), **{na: r, nb: SIDE - d})],
                )
    kept = []
    for i in (0,) + inward:
        for f in groups:
            _, nb, nc = fan_name[f]
            if i:
                for r in range(SIDE):
                    two[f, r, SIDE - i].wait_recv()
            for d in deltas:
                three.append(
                    send(
                        FANS[f][2],
                        d,
                        mids[f].at[spot(f, d, **{nb: i})],
                        arrived.at[place(f, **{nb: i, nc: SIDE - d})],
                    )
                )
            kept.append(
                move(mids[f].at[spot(f, 0, **{nb: i})], arrived.at[place(f, **{nb: i, nc: 0})])
            )
    for copy in three:
        copy.wait_recv()
    for copy in swapped:
        copy.wait_recv()
    for copy in own + kept:
        copy.wait()

    batch = rows.shape[0]
    width = rows.shape[1]
    chunk = 512
    contract = (((1,), (1,)), ((), ()))

    def ffn(j):
        rows[...] = arrived[j].astype(jnp.float32).reshape(batch, width).astype(jnp.bfloat16)

        @pl.loop(0, 2)
        def _(h):
            gate = lax.dot_general(
                rows[...], weights[h, 0], contract, preferred_element_type=jnp.float32
            )
            up = lax.dot_general(
                rows[...], weights[h, 1], contract, preferred_element_type=jnp.float32
            )
            act[h] = (gate / (1.0 + jnp.exp(-gate)) * up).astype(jnp.bfloat16)

        for n in range(0, width, chunk):
            cols = slice(n, n + chunk)
            total = jnp.dot(act[0], weights[0, 2, :, cols], preferred_element_type=jnp.float32)
            total += jnp.dot(act[1], weights[1, 2, :, cols], preferred_element_type=jnp.float32)
            total = total.reshape(result.shape[1:5] + (chunk,))
            result[j, :, :, :, :, cols] = total.astype(jnp.bfloat16)

    rets, homes = (ret0, ret1, ret2), (home0, home1, home2)
    parts, gots = (part0, part1, part2), (got0, got1, got2)
    back_one, back_two, back_three, stay, home = {}, {}, {}, {}, {}
    for j in (2, 1, 3, 0):
        ffn(j)
        for f in groups:
            axis = FANS[f][2]
            for d in (0,) + deltas:
                at = {"z": j}
                if axis == 0 and d != j:
                    continue
                if axis:
                    at[AXES[axis]] = d
                rest = {} if axis == 0 else {"z": j}
                source = result.at[place(f, **at)]
                if d:
                    back_one.setdefault((f, SIDE - d), []).append(
                        send(axis, d, source, rets[f].at[spot(f, SIDE - d, **rest)])
                    )
                else:
                    stay.setdefault(f, []).append(
                        move(source, rets[f].at[spot(f, 0, **rest)])
                    )
    for j in (0,) + inward:
        for f in groups:
            nb = fan_name[f][1]
            if j:
                for copy in back_one[f, j]:
                    copy.wait_recv()
            else:
                for copy in stay[f]:
                    copy.wait()
            for d in deltas:
                back_two.setdefault((f, SIDE - d), []).append(
                    send(
                        FANS[f][1],
                        d,
                        rets[f].at[spot(f, j, **{nb: d})],
                        homes[f].at[SIDE - d, j],
                    )
                )
            home.setdefault(f, []).append(
                move(rets[f].at[spot(f, j, **{nb: 0})], homes[f].at[0, j])
            )

    def blended(f, r):
        wide = SLICES[f][1]
        table = names[...] if r == 0 else far_names[f, r]
        held = homes[f][:, :, r].astype(jnp.float32)
        held = held.reshape(SIDE * SIDE * 24, wide).astype(jnp.bfloat16)
        return lax.dot_general(
            picks(table, f, True),
            held,
            (((0,), (0,)), ((), ())),
            preferred_element_type=jnp.float32,
        )

    for f in groups:
        for i in range(1, SIDE):
            for copy in back_two[f, i]:
                copy.wait_recv()
        for copy in home[f]:
            copy.wait()
        for r in deltas:
            parts[f][r] = blended(f, r).astype(jnp.bfloat16)
        for r in deltas:
            back_three[f, SIDE - r] = send(
                FANS[f][0], r, parts[f].at[r], gots[f].at[SIDE - r]
            )
    for f in groups:
        start, wide = SLICES[f]
        total = stream[:, start : start + wide] + blended(f, 0)
        for r in range(1, SIDE):
            back_three[f, r].wait_recv()
            total += gots[f][r].astype(jnp.float32)
        out[:, start : start + wide] = total.astype(out.dtype)
    for copy in sent:
        copy.wait_send()


def run_experts(normed, names, stream, gate_w, up_w, down_w):
    dtype = normed.dtype
    tokens = normed.shape[0]
    hidden, width = down_w.shape
    cells = (SIDE, SIDE, SIDE, 3, 8)
    batch = 3 * SIDE * SIDE * 8
    copies = 3 * (2 * 3 + 4 * 3 + 4 * 3) + 3 + (3 + 2 * 4 * 3) + 3 * (4 * 3 + 3)
    vmem = pl.BlockSpec(memory_space=pltpu.VMEM)
    hbm = pl.BlockSpec(memory_space=pl.ANY)
    return pl.pallas_call(
        expert_kernel,
        out_shape=jax.ShapeDtypeStruct((tokens, width), dtype),
        in_specs=[vmem, vmem, vmem, hbm, hbm, hbm],
        out_specs=vmem,
        scratch_shapes=[pltpu.VMEM((SIDE, tokens, wide), dtype) for _, wide in SLICES]
        + [pltpu.VMEM(cells + (wide,), dtype) for _, wide in SLICES]
        + [pltpu.VMEM(cells + (wide,), dtype) for _, wide in SLICES]
        + [
            pltpu.VMEM((3, SIDE, 16, tokens), jnp.float32),
            pltpu.VMEM(cells + (width,), dtype),
            pltpu.VMEM(cells + (width,), dtype),
        ]
        + [pltpu.VMEM(cells + (wide,), dtype) for _, wide in SLICES]
        + [pltpu.VMEM(cells + (wide,), dtype) for _, wide in SLICES]
        + [pltpu.VMEM((SIDE, tokens, wide), dtype) for _, wide in SLICES]
        + [pltpu.VMEM((SIDE, tokens, wide), dtype) for _, wide in SLICES]
        + [
            pltpu.VMEM((2, 3, hidden, width), dtype),
            pltpu.VMEM((batch, width), dtype),
            pltpu.VMEM((2, batch, hidden), dtype),
            pltpu.SemaphoreType.DMA((3 + 3 * 4 + (1 + 2 * 4) + 3 * 4,)),
            pltpu.SemaphoreType.DMA((copies,)),
            pltpu.SemaphoreType.DMA((copies,)),
        ],
        compiler_params=pltpu.CompilerParams(
            collective_id=0, has_side_effects=True, vmem_limit_bytes=60 << 20
        ),
        name="run_experts",
    )(normed, names, stream, gate_w, up_w, down_w)


def attention(queries, keys, values, pair_ids):
    tok_rows, local_width = queries.shape
    local_heads = local_width // HD
    shard = lax.axis_index("seq")
    widened = with_halo(jnp.stack([keys, values]), "seq", 1, tok_rows)
    id_pad = jnp.pad(pair_ids, (tok_rows, tok_rows), constant_values=-1)
    key_ids = lax.dynamic_slice_in_dim(id_pad, shard * tok_rows, 3 * tok_rows, 0)
    query_ids = lax.dynamic_slice_in_dim(id_pad, shard * tok_rows + tok_rows, tok_rows, 0)
    query_pos = jnp.arange(tok_rows, dtype=jnp.int32) + tok_rows
    key_pos = jnp.arange(3 * tok_rows, dtype=jnp.int32)
    allowed = (query_ids[:, None] == key_ids[None, :]) & (
        jnp.abs(query_pos[:, None] - key_pos[None, :]) < tok_rows
    )
    query_heads = queries.reshape(tok_rows, local_heads, HD)
    key_heads = widened[0].reshape(3 * tok_rows, local_heads, HD)
    value_heads = widened[1].reshape(3 * tok_rows, local_heads, HD)
    score = jnp.einsum(
        "qhd,khd->hqk", query_heads, key_heads, preferred_element_type=jnp.float32
    ) / math.sqrt(HD)
    score = jnp.where(allowed[None], score, -jnp.inf)
    top = jnp.max(score, axis=-1, keepdims=True)
    weights = jnp.exp(score - top)
    probs = (weights / jnp.sum(weights, axis=-1, keepdims=True)).astype(jnp.bfloat16)
    attended = jnp.einsum("hqk,khd->qhd", probs, value_heads, preferred_element_type=jnp.float32)
    return attended.reshape(tok_rows, local_width).astype(jnp.bfloat16)


def shards(
    queries,
    keys,
    values,
    resid,
    pair_ids,
    out_weight,
    norm_gain,
    experts,
    gates,
    w_gate,
    w_up,
    w_down,
):
    moe_rows = resid.shape[0]
    core = lax.axis_index("exp")
    attended = attention(queries, keys, values, pair_ids)
    mine = lax.dynamic_slice_in_dim(attended, core * moe_rows, moe_rows, 0)
    yours = swap(lax.dynamic_slice_in_dim(attended, (1 - core) * moe_rows, moe_rows, 0))
    out_other = swap(out_weight)
    stream = (
        resid.astype(jnp.float32)
        + jnp.dot(mine, out_weight, preferred_element_type=jnp.float32)
        + jnp.dot(yours, out_other, preferred_element_type=jnp.float32)
    )
    meansq = jnp.mean(stream * stream, axis=-1, keepdims=True)
    normed = (stream * lax.rsqrt(meansq + 1e-05) * norm_gain).astype(jnp.bfloat16)
    lines = ((0, 8 - TOP), (0, 0))
    names = jnp.concatenate(
        [
            jnp.pad(experts.T.astype(jnp.float32), lines, constant_values=-1.0),
            jnp.pad(gates.T, lines),
        ]
    )
    return run_experts(normed, names, stream, w_gate[0].T, w_up[0].T, w_down[0])


def solution(mesh):
    in_specs = (
        P("seq", "exp"),
        P("seq", "exp"),
        P("seq", "exp"),
        P(("seq", "exp"), None),
        P(),
        P("exp", None),
        P(),
        P(("seq", "exp"), None),
        P(("seq", "exp"), None),
        P("seq", None, "exp"),
        P("seq", None, "exp"),
        P("seq", "exp", None),
    )
    out_specs = P(("seq", "exp"), None)
    return jax.shard_map(shards, mesh=mesh, in_specs=in_specs, out_specs=out_specs, check_vma=False)
```
